128 devices in a mesh: ep: 8 (over y, core), tp: 16 (over z, x).
Axes of the slice: x: 4, y: 4, z: 4, core: 2. Of those that a mesh axis runs over, the one named last changes fastest.
Arguments:
- query_key_value: bfloat16 [32, 512, 3, 1792], P('ep', 'tp'), may hold values from -6 to 6
- residual: bfloat16 [32, 512, 1792], P('ep', 'tp'), may hold values from -6 to 6
- norm_gain: float32 [1792], replicated, may hold values from 0.1 to 1.9
- expert_ids: int32 [32, 512, 2], P('ep', 'tp'), may hold values from 0 to 15, as said below
- route_gates: float32 [32, 512, 2], P('ep', 'tp'), may hold values from 0.2 to 1
- slot_index: int32 [32, 512, 2], P('ep', 'tp'), may hold values from -1 to 15, as said below
- w_gate: bfloat16 [16, 1792, 7168], P('ep', None, 'tp'), may hold values from -0.125 to 0.125
- w_up: bfloat16 [16, 1792, 7168], P('ep', None, 'tp'), may hold values from -0.125 to 0.125
- w_down: bfloat16 [16, 7168, 1792], P('ep', 'tp'), may hold values from -0.0625 to 0.0625
Outputs:
- block_out: bfloat16 [32, 512, 1792], P('ep', 'tp')
The draws below stay inside these ranges and needn't reach their ends.
Inputs may be any that keep to these rules, and one draw needn't show every extreme that they name: `expert_ids`: each token names two different experts. One expert is the first choice of 16 or more tokens of every device (a device holds 4 frames by 32 sites). `slot_index`: the rank of an assignment among the assignments of the same expert on the same device, counted in the order frame, site, choice; -1 where that rank is 16 or more. Every device fills all 16 slots of some expert.
All inputs are finite; a program needn't handle non-finite values.
Results may differ from the reference program's by a relative error of at most 0.0095.
Values may be sent and summed in bfloat16 or wider, within the bound.
No kernel may reach another device: no remote copies, remote signals or barrier semaphores. Data moves between devices by JAX's collectives and lax.ppermute only.
A program may use at most 128 MiB of HBM per device.

```python
import math
import jax
import jax.numpy as jnp
from jax import lax

D = 1792
HD = 64
HEADS = 28
FF = 7168
EXPERTS = 16
FR_DEV = 4
SITE_DEV = 32
FRAMES = 32
SITES = 512
TOK_DEV = 128
CAP = 16
FF_DEV = 448
N_EP = 8
N_TP = 16


def draw_query_key_value(key, part):
    keys = jax.random.split(key, 1)
    shape = (FRAMES, SITES, 3, D)
    values = jnp.clip(jax.random.normal(keys[0], shape, jnp.float32), -6.0, 6.0)
    return values.astype(jnp.bfloat16)


def to_blocks(array):
    rows_ep = FRAMES // FR_DEV
    rows_tp = SITES // SITE_DEV
    return array.reshape(rows_ep, FR_DEV, rows_tp, SITE_DEV).transpose(0, 2, 1, 3).reshape(rows_ep, rows_tp, TOK_DEV)


def from_blocks(array):
    rows_ep = FRAMES // FR_DEV
    rows_tp = SITES // SITE_DEV
    shaped = array.reshape(rows_ep, rows_tp, FR_DEV, SITE_DEV, 2)
    return shaped.transpose(0, 2, 1, 3, 4).reshape(FRAMES, SITES, 2)


def routing(key):
    key = jax.random.fold_in(key, 7)
    keys = jax.random.split(key, 5)
    grid = (FRAMES, SITES)
    first = jax.random.randint(keys[0], grid, 0, EXPERTS) * jax.random.randint(keys[1], grid, 0, EXPERTS) // EXPERTS
    offset = jax.random.randint(keys[2], grid, 1, EXPERTS)
    order = jax.random.permutation(keys[3], EXPERTS).astype(jnp.int32)
    noise = jax.random.randint(keys[4], grid, 0, 1 << 20)
    local = (jnp.arange(FRAMES, dtype=jnp.int32) % FR_DEV)[:, None] * SITE_DEV + (jnp.arange(SITES, dtype=jnp.int32) % SITE_DEV)[None, :]
    score = to_blocks(noise * TOK_DEV + local)
    ranking = jnp.argsort(jnp.argsort(score, axis=-1), axis=-1)
    forced = ranking < CAP
    first_b = jnp.where(forced, 0, to_blocks(first))
    second_b = (first_b + to_blocks(offset)) % EXPERTS
    ids_b = order[jnp.stack([first_b, second_b], axis=-1)]
    flat = ids_b.reshape(ids_b.shape[0], ids_b.shape[1], TOK_DEV * 2)
    hits = (flat[..., None] == jnp.arange(EXPERTS, dtype=jnp.int32)).astype(jnp.int32)
    seen = jnp.cumsum(hits, axis=2) - hits
    position = jnp.sum(seen * hits, axis=-1)
    slots_b = jnp.where(position < CAP, position, -1).astype(jnp.int32)
    return (from_blocks(ids_b).astype(jnp.int32), from_blocks(slots_b).astype(jnp.int32))


def draw_expert_ids(key, part):
    return routing(key)[0]


def draw_slot_index(key, part):
    return routing(key)[1]


def block_scale(key, extent, cuts, low, top_value):
    def one(dim, parts):
        heights = jax.random.uniform(jax.random.fold_in(jax.random.fold_in(key, 6), dim), (parts,), jnp.float32, low / len(cuts), top_value / len(cuts))
        return jnp.repeat(jnp.exp(heights), extent[dim] // parts).reshape((-1,) + (1,) * (len(extent) - dim - 1))

    gain = one(*cuts[0])
    for cut in cuts[1:]:
        gain = gain * one(*cut)
    return gain


def bell_draw(key, dims, width, reach, cuts=(), kind=jnp.bfloat16):
    drawn = jax.random.normal(key, dims, jnp.float32) * width
    if len(cuts) > 0:
        drawn = block_scale(key, dims, cuts, -0.22, 0.18) * drawn
    return jnp.clip(drawn, min=-reach, max=reach).astype(kind)


def setup_inputs(seed: int = 0) -> dict:
    streams_of = jax.random.split(jax.random.key(seed), 10)
    query_key_value = draw_query_key_value(jax.random.fold_in(streams_of[9], 71), 0)
    residual = bell_draw(streams_of[1], (FRAMES, SITES, D), 1.0, 6.0, ((0, 8), (1, 16)))
    norm_gain = jnp.clip(1.0 + 0.18 * jax.random.normal(streams_of[2], (D,), jnp.float32), 0.1, 1.9)
    expert_ids = draw_expert_ids(jax.random.fold_in(streams_of[9], 71), 0)
    route_gates = jnp.clip(0.2 + 0.8 * jax.random.uniform(streams_of[4], (FRAMES, SITES, 2), jnp.float32) ** block_scale(streams_of[4], (FRAMES, SITES, 2), ((0, 8), (1, 16)), -0.2, 0.2), 0.2, 1.0)
    slot_index = draw_slot_index(jax.random.fold_in(streams_of[9], 71), 0)
    w_gate = bell_draw(streams_of[6], (EXPERTS, D, FF), D ** -0.5, 0.125, ((0, 8), (2, 16)))
    w_up = bell_draw(streams_of[7], (EXPERTS, D, FF), D ** -0.5, 0.125, ((0, 8), (2, 16)))
    w_down = bell_draw(streams_of[8], (EXPERTS, FF, D), FF ** -0.5, 0.0625, ((0, 8), (1, 16)))
    return dict(query_key_value=query_key_value, residual=residual, norm_gain=norm_gain, expert_ids=expert_ids, route_gates=route_gates, slot_index=slot_index, w_gate=w_gate, w_up=w_up, w_down=w_down)


def attend(query_part, key_part, value_part):
    frames_q, site_count, model_width = query_part.shape
    frames_k = key_part.shape[0]
    query_h = query_part.astype(jnp.float32).reshape(frames_q, site_count, HEADS, HD)
    key_h = key_part.astype(jnp.float32).reshape(frames_k, site_count, HEADS, HD)
    value_h = value_part.astype(jnp.float32).reshape(frames_k, site_count, HEADS, HD)
    scores = jnp.einsum('fshd,gshd->shfg', query_h, key_h) / math.sqrt(HD)
    scores = scores - lax.optimization_barrier(jnp.max(scores, axis=-1, keepdims=True))
    expo = jnp.exp(scores)
    probs = (expo / lax.optimization_barrier(jnp.sum(expo, axis=-1, keepdims=True))).astype(jnp.bfloat16)
    mixed = jnp.einsum('shfg,gshd->fshd', probs.astype(jnp.float32), value_h)
    return mixed.reshape(frames_q, site_count, model_width).astype(jnp.bfloat16)

def reference(query_key_value, residual, norm_gain, expert_ids, route_gates, slot_index, w_gate, w_up, w_down):
    attended = attend(query_key_value[:, :, 0], query_key_value[:, :, 1], query_key_value[:, :, 2])
    hidden = residual.astype(jnp.float32) + attended.astype(jnp.float32)
    scale = lax.rsqrt(lax.optimization_barrier(jnp.mean(hidden * hidden, axis=-1, keepdims=True)) + 1e-06)
    normed = (hidden * scale * norm_gain).astype(jnp.bfloat16)
    frame_idx = jnp.arange(FRAMES, dtype=jnp.int32)[:, None]
    site_idx = jnp.arange(SITES, dtype=jnp.int32)[None, :]
    device = frame_idx // FR_DEV * N_TP + site_idx // SITE_DEV
    valid = slot_index >= 0
    row_pos = (device[:, :, None] * CAP + slot_index).astype(jnp.int32)
    total_rows = N_EP * N_TP * CAP
    target = jnp.where(valid, row_pos, total_rows).astype(jnp.int32)
    spread = jnp.broadcast_to(normed[:, :, None, :], (FRAMES, SITES, 2, D))
    buffers = jnp.zeros((EXPERTS, total_rows, D), jnp.bfloat16).at[expert_ids, target].set(spread, mode='drop')

    def run_expert(operands):
        rows_in, gate_mat, up_mat, down_mat = operands
        gate_val = jnp.dot(rows_in, gate_mat, preferred_element_type=jnp.float32)
        up_val = jnp.dot(rows_in, up_mat, preferred_element_type=jnp.float32)
        active = (jax.nn.silu(gate_val) * up_val).astype(jnp.bfloat16)
        active_blocks = active.reshape(total_rows, N_TP, FF_DEV).transpose(1, 0, 2)
        down_blocks = down_mat.reshape(N_TP, FF_DEV, D)

        def add_block(carry, pair):
            part = jnp.dot(pair[0], pair[1], preferred_element_type=jnp.float32).astype(jnp.bfloat16)
            part = lax.optimization_barrier(part)
            return (carry + part.astype(jnp.float32), None)
        total, _ = lax.scan(add_block, jnp.zeros((total_rows, D), jnp.float32), (active_blocks, down_blocks))
        return total.astype(jnp.bfloat16)
    outputs = lax.map(run_expert, (buffers, w_gate, w_up, w_down))
    picked = outputs[expert_ids, jnp.where(valid, row_pos, 0).astype(jnp.int32)]
    weights = jnp.where(valid, route_gates, 0.0)
    combined = hidden + lax.optimization_barrier(jnp.sum(weights[..., None] * picked.astype(jnp.float32), axis=2))
    return combined.astype(jnp.bfloat16)
```

```python
import math

import jax
import jax.numpy as jnp
from jax import lax
from jax.experimental import pallas as pl
from jax.experimental.pallas import tpu as pltpu
from jax.sharding import PartitionSpec as P

HD = 64
SITE_GROUP = 8
LANES = 2 * HD


def nt_dot(left, right):
    return lax.dot_general(
        left, right, (((1,), (1,)), ((), ())), preferred_element_type=jnp.float32
    )


def attend_kernel(qkv_ref, out_ref):
    sources, _, frames, sites, width = qkv_ref.shape
    rows = sources * frames * sites
    row_site = lax.broadcasted_iota(jnp.int32, (2 * rows, rows), 0) % sites
    col_site = lax.broadcasted_iota(jnp.int32, (2 * rows, rows), 1) % sites
    same_site = row_site == col_site
    low_head = lax.broadcasted_iota(jnp.int32, (rows, LANES), 1) < HD
    for pair in range(width // LANES):
        cols = pl.ds(pair * LANES, LANES)
        query = qkv_ref[:, 0, :, :, cols].reshape(rows, LANES)
        key = qkv_ref[:, 1, :, :, cols].reshape(rows, LANES)
        value = qkv_ref[:, 2, :, :, cols].reshape(rows, LANES)
        zero = jnp.zeros_like(query)
        both = jnp.concatenate(
            [jnp.where(low_head, query, zero), jnp.where(low_head, zero, query)], axis=0
        )
        scores = nt_dot(both, key) * (1.0 / math.sqrt(HD))
        scores = jnp.where(same_site, scores, -jnp.inf)
        expo = jnp.exp(scores - jnp.max(scores, axis=-1, keepdims=True))
        probs = (expo / jnp.sum(expo, axis=-1, keepdims=True)).astype(jnp.bfloat16)
        mixed = jnp.dot(probs, value, preferred_element_type=jnp.float32)
        mixed = jnp.where(low_head, mixed[:rows], mixed[rows:])
        out_ref[:, :, :, cols] = mixed.astype(out_ref.dtype).reshape(
            sources, frames, sites, LANES
        )


def route_kernel(att_ref, res_ref, gain_ref, target_ref, hidden_ref, first_ref, second_ref):
    _, frames, sites, half = att_ref.shape
    groups = att_ref.shape[0] // 2
    tokens = frames * groups * sites
    attended = jnp.concatenate(
        [
            jnp.concatenate(
                [
                    att_ref[2 * group + side, frame].astype(jnp.float32)
                    for frame in range(frames)
                    for group in range(groups)
                ],
                axis=0,
            )
            for side in range(2)
        ],
        axis=1,
    )
    hidden = res_ref[...].reshape(tokens, 2 * half).astype(jnp.float32) + attended
    hidden_ref[...] = hidden
    scale = lax.rsqrt(jnp.mean(hidden * hidden, axis=-1, keepdims=True) + 1e-06)
    normed = (hidden * scale * gain_ref[...]).astype(jnp.bfloat16)
    slots = first_ref.shape[0]
    for index, out in enumerate((first_ref, second_ref)):
        row = lax.broadcasted_iota(jnp.int32, (slots, tokens), 0) + index * slots
        hit = (row == target_ref[0:1, :]) | (row == target_ref[1:2, :])
        picker = jnp.where(hit, 1.0, 0.0).astype(jnp.bfloat16)
        out[...] = jnp.dot(picker, normed, preferred_element_type=jnp.float32).astype(
            jnp.bfloat16
        )


def combine_kernel(hidden_ref, first_ref, second_ref, target_ref, gate_ref, out_ref):
    tokens = hidden_ref.shape[0]
    slots = first_ref.shape[0]
    returned = jnp.concatenate([first_ref[...], second_ref[...]], axis=0)
    col = lax.broadcasted_iota(jnp.int32, (tokens, 2 * slots), 1)
    moved = jnp.zeros(hidden_ref.shape, jnp.float32)
    for choice in range(2):
        target = target_ref[:, choice : choice + 1]
        picker = jnp.where(col == target, 1.0, 0.0).astype(jnp.bfloat16)
        weight = jnp.where(target >= 0, gate_ref[:, choice : choice + 1], 0.0)
        moved = moved + weight * jnp.dot(picker, returned, preferred_element_type=jnp.float32)
    out_ref[...] = (hidden_ref[...] + moved).astype(out_ref.dtype)


def body(
    query_key_value, residual, norm_gain, expert_ids, route_gates, slot_index, w_gate, w_up, w_down
):
    frames_local, sites_local, model_width = residual.shape
    groups = lax.axis_size("ep")
    halves = 2
    site_groups = sites_local // SITE_GROUP
    assert site_groups * halves == groups
    half = model_width // halves
    tokens = frames_local * sites_local
    experts_local = w_gate.shape[0]
    experts_all = experts_local * groups
    capacity = 2 * tokens // experts_all
    bf16 = jnp.bfloat16

    spread = query_key_value.reshape(
        frames_local, site_groups, SITE_GROUP, 3, halves, half
    ).transpose(1, 4, 3, 0, 2, 5)
    spread = spread.reshape(groups, 3, frames_local, SITE_GROUP, half)
    together = lax.all_to_all(spread, "ep", split_axis=0, concat_axis=0, tiled=True)
    mixed = pl.pallas_call(
        attend_kernel,
        out_shape=jax.ShapeDtypeStruct((groups, frames_local, SITE_GROUP, half), bf16),
        name="attend",
    )(together)
    attended = lax.all_to_all(mixed, "ep", split_axis=0, concat_axis=0, tiled=True)

    row_of = (expert_ids % experts_local) * (groups * capacity) + (
        expert_ids // experts_local
    ) * capacity
    target = jnp.where(slot_index >= 0, row_of + slot_index, -1).reshape(tokens, 2)
    gates = route_gates.reshape(tokens, 2)
    slots = groups * capacity
    hidden, first, second = pl.pallas_call(
        route_kernel,
        out_shape=(
            jax.ShapeDtypeStruct((tokens, model_width), jnp.float32),
            jax.ShapeDtypeStruct((slots, model_width), bf16),
            jax.ShapeDtypeStruct((slots, model_width), bf16),
        ),
        name="route",
    )(attended, residual, norm_gain.reshape(1, model_width), target.T)

    def expert(index, outgoing):
        arrived = lax.all_to_all(outgoing, "ep", split_axis=0, concat_axis=0, tiled=True)
        gathered = lax.all_gather(arrived, "tp", axis=0, tiled=True)
        gate_val = jnp.dot(gathered, w_gate[index], preferred_element_type=jnp.float32)
        up_val = jnp.dot(gathered, w_up[index], preferred_element_type=jnp.float32)
        active = (jax.nn.silu(gate_val) * up_val).astype(bf16)
        partial = jnp.dot(active, w_down[index], preferred_element_type=jnp.float32).astype(bf16)
        summed = lax.psum_scatter(partial, "tp", scatter_dimension=0, tiled=True)
        return lax.all_to_all(summed, "ep", split_axis=0, concat_axis=0, tiled=True)

    back = [expert(0, first), expert(1, second)]
    combined = pl.pallas_call(
        combine_kernel,
        out_shape=jax.ShapeDtypeStruct((tokens, model_width), bf16),
        name="combine",
    )(hidden, back[0], back[1], target, gates)
    return combined.reshape(frames_local, sites_local, model_width)


def solution(mesh):
    return jax.shard_map(
        body,
        mesh=mesh,
        in_specs=(
            P("ep", "tp", None, None),
            P("ep", "tp", None),
            P(),
            P("ep", "tp", None),
            P("ep", "tp", None),
            P("ep", "tp", None),
            P("ep", None, "tp"),
            P("ep", None, "tp"),
            P("ep", "tp", None),
        ),
        out_specs=P("ep", "tp", None),
        check_vma=False,
    )
```

```python
import math

import jax
import jax.numpy as jnp
from jax import lax
from jax.experimental import pallas as pl
from jax.experimental.pallas import tpu as pltpu
from jax.sharding import PartitionSpec as P

HD = 64
SITE_GROUP = 8
LANES = 2 * HD
SIDE = 4


def nt_dot(left, right):
    return lax.dot_general(
        left, right, (((1,), (1,)), ((), ())), preferred_element_type=jnp.float32
    )


def attend_kernel(qkv_ref, out_ref):
    sources, _, frames, sites, width = qkv_ref.shape
    rows = sources * frames * sites
    row_site = lax.broadcasted_iota(jnp.int32, (2 * rows, rows), 0) % sites
    col_site = lax.broadcasted_iota(jnp.int32, (2 * rows, rows), 1) % sites
    same_site = row_site == col_site
    low_head = lax.broadcasted_iota(jnp.int32, (rows, LANES), 1) < HD
    for pair in range(width // LANES):
        cols = pl.ds(pair * LANES, LANES)
        query = qkv_ref[:, 0, :, :, cols].reshape(rows, LANES)
        key = qkv_ref[:, 1, :, :, cols].reshape(rows, LANES)
        value = qkv_ref[:, 2, :, :, cols].reshape(rows, LANES)
        zero = jnp.zeros_like(query)
        both = jnp.concatenate(
            [jnp.where(low_head, query, zero), jnp.where(low_head, zero, query)], axis=0
        )
        scores = nt_dot(both, key) * (1.0 / math.sqrt(HD))
        scores = jnp.where(same_site, scores, -jnp.inf)
        expo = jnp.exp(scores - jnp.max(scores, axis=-1, keepdims=True))
        probs = (expo / jnp.sum(expo, axis=-1, keepdims=True)).astype(jnp.bfloat16)
        mixed = jnp.dot(probs, value, preferred_element_type=jnp.float32)
        mixed = jnp.where(low_head, mixed[:rows], mixed[rows:])
        out_ref[:, :, :, cols] = mixed.astype(out_ref.dtype).reshape(
            sources, frames, sites, LANES
        )


def route_kernel(att_ref, res_ref, gain_ref, target_ref, hidden_ref, rows_ref):
    _, frames, sites, half = att_ref.shape
    groups = att_ref.shape[0] // 2
    tokens = frames * groups * sites
    attended = jnp.concatenate(
        [
            jnp.concatenate(
                [
                    att_ref[2 * group + side, frame].astype(jnp.float32)
                    for frame in range(frames)
                    for group in range(groups)
                ],
                axis=0,
            )
            for side in range(2)
        ],
        axis=1,
    )
    hidden = res_ref[...].reshape(tokens, 2 * half).astype(jnp.float32) + attended
    hidden_ref[...] = hidden
    scale = lax.rsqrt(jnp.mean(hidden * hidden, axis=-1, keepdims=True) + 1e-06)
    normed = (hidden * scale * gain_ref[...]).astype(jnp.bfloat16)
    row = lax.broadcasted_iota(jnp.int32, (rows_ref.shape[0], tokens), 0)
    hit = (row == target_ref[0:1, :]) | (row == target_ref[1:2, :])
    picker = jnp.where(hit, 1.0, 0.0).astype(jnp.bfloat16)
    rows_ref[...] = jnp.dot(picker, normed, preferred_element_type=jnp.float32).astype(
        jnp.bfloat16
    )


def combine_kernel(hidden_ref, rows_ref, target_ref, gate_ref, out_ref):
    tokens = hidden_ref.shape[0]
    returned = rows_ref[...]
    col = lax.broadcasted_iota(jnp.int32, (tokens, returned.shape[0]), 1)
    moved = jnp.zeros(hidden_ref.shape, jnp.float32)
    for choice in range(2):
        target = target_ref[:, choice : choice + 1]
        picker = jnp.where(col == target, 1.0, 0.0).astype(jnp.bfloat16)
        weight = jnp.where(target >= 0, gate_ref[:, choice : choice + 1], 0.0)
        moved = moved + weight * jnp.dot(picker, returned, preferred_element_type=jnp.float32)
    out_ref[...] = (hidden_ref[...] + moved).astype(out_ref.dtype)


def mlp_kernel(
    rows_ref, gate_a, up_a, down_a, gate_b, up_b, down_b, out_ref, acc_ref
):
    rows = rows_ref[...]
    total = None
    for gate_ref, up_ref, down_ref in ((gate_a, up_a, down_a), (gate_b, up_b, down_b)):
        gate_val = nt_dot(rows, gate_ref[...])
        up_val = nt_dot(rows, up_ref[...])
        active = (gate_val / (1.0 + jnp.exp(-gate_val)) * up_val).astype(jnp.bfloat16)
        part = jnp.dot(active, down_ref[...], preferred_element_type=jnp.float32)
        total = part if total is None else total + part
    step = pl.program_id(0)

    @pl.when(step == 0)
    def _():
        acc_ref[...] = total

    @pl.when(step > 0)
    def _():
        acc_ref[...] += total

    @pl.when(step == pl.num_programs(0) - 1)
    def _():
        out_ref[...] = acc_ref[...].astype(out_ref.dtype)


def mlp(rows, index, gate, up, down, near):
    count, width = rows.shape
    hidden_units = gate.shape[1]
    steps = 2
    block = hidden_units // steps
    own = pl.BlockSpec((None, block, width), lambda i: (index, i, 0))
    whole = pl.BlockSpec((count, width), lambda i: (0, 0))

    def other(which):
        return pl.BlockSpec((None, block, width), lambda i: (which, i, 0))

    return pl.pallas_call(
        mlp_kernel,
        grid=(steps,),
        in_specs=[whole, own, own, own, other(0), other(1), other(2)],
        out_specs=whole,
        out_shape=jax.ShapeDtypeStruct((count, width), jnp.bfloat16),
        scratch_shapes=[pltpu.VMEM((count, width), jnp.float32)],
        name="mlp",
    )(rows, gate, up, down, near, near, near)


def hop(sizes, move):
    count_y, count_z, count_x = sizes

    def index(y, c, z, x):
        return (
            ((y % count_y) * 2 + c) * (count_z * count_x)
            + (z % count_z) * count_x
            + x % count_x
        )

    return [
        (index(y, c, z, x), index(*move(y, c, z, x)))
        for y in range(count_y)
        for c in range(2)
        for z in range(count_z)
        for x in range(count_x)
    ]


def body(
    query_key_value, residual, norm_gain, expert_ids, route_gates, slot_index, w_gate, w_up, w_down
):
    frames_local, sites_local, model_width = residual.shape
    groups = lax.axis_size("ep")
    halves = 2
    site_groups = sites_local // SITE_GROUP
    assert site_groups * halves == groups
    half = model_width // halves
    tokens = frames_local * sites_local
    experts_local = w_gate.shape[0]
    experts_all = experts_local * groups
    capacity = 2 * tokens // experts_all
    bf16 = jnp.bfloat16

    spread = query_key_value.reshape(
        frames_local, site_groups, SITE_GROUP, 3, halves, half
    ).transpose(1, 4, 3, 0, 2, 5)
    spread = spread.reshape(groups, 3, frames_local, SITE_GROUP, half)
    together = lax.all_to_all(spread, "ep", split_axis=0, concat_axis=0, tiled=True)
    mixed = pl.pallas_call(
        attend_kernel,
        out_shape=jax.ShapeDtypeStruct((groups, frames_local, SITE_GROUP, half), bf16),
        name="attend",
    )(together)
    attended = lax.all_to_all(mixed, "ep", split_axis=0, concat_axis=0, tiled=True)

    sizes = (groups // 2, SIDE, lax.axis_size("tp") // SIDE)

    def along_x(steps):
        return hop(sizes, lambda y, c, z, x: (y, c, z, x + steps))

    def along_z(steps):
        return hop(sizes, lambda y, c, z, x: (y, c, z + steps, x))

    def send(value, pairs):
        return lax.ppermute(value, ("ep", "tp"), pairs)

    gate = w_gate.transpose(0, 2, 1)
    up = w_up.transpose(0, 2, 1)
    near = [
        send(
            jnp.stack([gate[0], up[0], w_down[0]]),
            hop(sizes, lambda y, c, z, x: (y, c, z, x - 1 + 2 * c)),
        ),
        send(
            jnp.stack([gate[1], up[1], w_down[1]]),
            hop(sizes, lambda y, c, z, x: (y, c, z - 1 + 2 * c, x)),
        ),
    ]

    target = jnp.where(slot_index >= 0, expert_ids * capacity + slot_index, -1)
    target = target.reshape(tokens, 2)
    gates = route_gates.reshape(tokens, 2)
    slots = experts_all * capacity
    hidden, rows = pl.pallas_call(
        route_kernel,
        out_shape=(
            jax.ShapeDtypeStruct((tokens, model_width), jnp.float32),
            jax.ShapeDtypeStruct((slots, model_width), bf16),
        ),
        name="route",
    )(attended, residual, norm_gain.reshape(1, model_width), target.T)
    arrived = lax.all_to_all(
        rows.reshape(groups, experts_local, capacity, model_width),
        "ep",
        split_axis=0,
        concat_axis=0,
        tiled=True,
    )
    block = groups * capacity
    mine = [arrived[:, e].reshape(block, model_width) for e in range(2)]
    far = (along_x, along_z)
    ring = (along_z, along_x)
    here = [jnp.concatenate([mine[e], send(mine[e], far[e](2))]) for e in range(2)]
    got = {}
    for step in (1, -1, 2):
        for e in range(2):
            got[e, step] = send(here[e], ring[e](step))
    parts = {e: [mlp(here[e], e, gate, up, w_down, near[e])] for e in range(2)}
    for step in (1, -1, 2):
        for e in range(2):
            part = mlp(got[e, step], e, gate, up, w_down, near[e])
            parts[e].append(send(part, ring[e](-step)))

    def add(pieces):
        total = pieces[0].astype(jnp.float32)
        for piece in pieces[1:]:
            total = total + piece.astype(jnp.float32)
        return total.astype(bf16)

    summed = []
    for e in range(2):
        opposite = add([part[block:] for part in parts[e]])
        summed.append(add([part[:block] for part in parts[e]] + [send(opposite, far[e](2))]))
    ready = jnp.stack([part.reshape(groups, capacity, model_width) for part in summed], axis=1)
    back = lax.all_to_all(ready, "ep", split_axis=0, concat_axis=0, tiled=True)
    combined = pl.pallas_call(
        combine_kernel,
        out_shape=jax.ShapeDtypeStruct((tokens, model_width), bf16),
        name="combine",
    )(hidden, back.reshape(slots, model_width), target, gates)
    return combined.reshape(frames_local, sites_local, model_width)


def solution(mesh):
    return jax.shard_map(
        body,
        mesh=mesh,
        in_specs=(
            P("ep", "tp", None, None),
            P("ep", "tp", None),
            P(),
            P("ep", "tp", None),
            P("ep", "tp", None),
            P("ep", "tp", None),
            P("ep", None, "tp"),
            P("ep", None, "tp"),
            P("ep", "tp", None),
        ),
        out_specs=P("ep", "tp", None),
        check_vma=False,
    )
```

```python
import math

import jax
import jax.numpy as jnp
from jax import lax
from jax.experimental import pallas as pl
from jax.experimental.pallas import tpu as pltpu
from jax.sharding import PartitionSpec as P


HD = 64
SITE_GROUP = 8
LANES = 2 * HD
SIDE = 4


def nt_dot(left, right):
    return lax.dot_general(
        left, right, (((1,), (1,)), ((), ())), preferred_element_type=jnp.float32
    )


def attend_kernel(qkv_ref, out_ref):
    sources, _, frames, sites, width = qkv_ref.shape
    rows = sources * frames * sites
    row_site = lax.broadcasted_iota(jnp.int32, (2 * rows, rows), 0) % sites
    col_site = lax.broadcasted_iota(jnp.int32, (2 * rows, rows), 1) % sites
    same_site = row_site == col_site
    low_head = lax.broadcasted_iota(jnp.int32, (rows, LANES), 1) < HD
    for pair in range(width // LANES):
        cols = pl.ds(pair * LANES, LANES)
        query = qkv_ref[:, 0, :, :, cols].reshape(rows, LANES)
        key = qkv_ref[:, 1, :, :, cols].reshape(rows, LANES)
        value = qkv_ref[:, 2, :, :, cols].reshape(rows, LANES)
        zero = jnp.zeros_like(query)
        both = jnp.concatenate(
            [jnp.where(low_head, query, zero), jnp.where(low_head, zero, query)], axis=0
        )
        scores = nt_dot(both, key) * (1.0 / math.sqrt(HD))
        scores = jnp.where(same_site, scores, -jnp.inf)
        expo = jnp.exp(scores - jnp.max(scores, axis=-1, keepdims=True))
        probs = (expo / jnp.sum(expo, axis=-1, keepdims=True)).astype(jnp.bfloat16)
        mixed = jnp.dot(probs, value, preferred_element_type=jnp.float32)
        mixed = jnp.where(low_head, mixed[:rows], mixed[rows:])
        out_ref[:, :, :, cols] = mixed.astype(out_ref.dtype).reshape(
            sources, frames, sites, LANES
        )


def route_kernel(att_ref, res_ref, gain_ref, target_ref, hidden_ref, rows_ref):
    _, frames, sites, half = att_ref.shape
    groups = att_ref.shape[0] // 2
    tokens = frames * groups * sites
    attended = jnp.concatenate(
        [
            jnp.concatenate(
                [
                    att_ref[2 * group + side, frame].astype(jnp.float32)
                    for frame in range(frames)
                    for group in range(groups)
                ],
                axis=0,
            )
            for side in range(2)
        ],
        axis=1,
    )
    hidden = res_ref[...].reshape(tokens, 2 * half).astype(jnp.float32) + attended
    hidden_ref[...] = hidden
    scale = lax.rsqrt(jnp.mean(hidden * hidden, axis=-1, keepdims=True) + 1e-06)
    normed = (hidden * scale * gain_ref[...]).astype(jnp.bfloat16)
    row = lax.broadcasted_iota(jnp.int32, (rows_ref.shape[0], tokens), 0)
    hit = (row == target_ref[0:1, :]) | (row == target_ref[1:2, :])
    picker = jnp.where(hit, 1.0, 0.0).astype(jnp.bfloat16)
    rows_ref[...] = jnp.dot(picker, normed, preferred_element_type=jnp.float32).astype(
        jnp.bfloat16
    )


def combine_kernel(hidden_ref, rows_ref, target_ref, gate_ref, out_ref):
    tokens = hidden_ref.shape[0]
    returned = rows_ref[...]
    col = lax.broadcasted_iota(jnp.int32, (tokens, returned.shape[0]), 1)
    moved = jnp.zeros(hidden_ref.shape, jnp.float32)
    for choice in range(2):
        target = target_ref[:, choice : choice + 1]
        picker = jnp.where(col == target, 1.0, 0.0).astype(jnp.bfloat16)
        weight = jnp.where(target >= 0, gate_ref[:, choice : choice + 1], 0.0)
        moved = moved + weight * jnp.dot(picker, returned, preferred_element_type=jnp.float32)
    out_ref[...] = (hidden_ref[...] + moved).astype(out_ref.dtype)


def mlp_kernel(index, pieces, *refs):
    rows_in = refs[:pieces]
    gate, up, down, near = refs[pieces : pieces + 4]
    outs = refs[pieces + 4 : 2 * pieces + 4]
    rows_buf, weight_buf, row_sem, weight_sem = refs[2 * pieces + 4 :]
    count = outs[0].shape[0]
    row_copies = [
        pltpu.make_async_copy(
            rows_in[i], rows_buf.at[pl.ds(i * count, count)], row_sem.at[i]
        )
        for i in range(pieces)
    ]
    sources = (
        gate.at[index],
        up.at[index],
        near.at[0],
        near.at[1],
        down.at[index],
        near.at[2],
    )
    weight_copies = [
        pltpu.make_async_copy(source, weight_buf.at[i], weight_sem.at[i])
        for i, source in enumerate(sources)
    ]
    for copy in row_copies + weight_copies:
        copy.start()
    for copy in row_copies:
        copy.wait()
    rows = rows_buf[...]
    actives = []
    for slice_index in range(2):
        weight_copies[2 * slice_index].wait()
        gate_val = nt_dot(rows, weight_buf[2 * slice_index])
        weight_copies[2 * slice_index + 1].wait()
        up_val = nt_dot(rows, weight_buf[2 * slice_index + 1])
        actives.append(
            (gate_val / (1.0 + jnp.exp(-gate_val)) * up_val).astype(jnp.bfloat16)
        )
    weight_copies[4].wait()
    total = jnp.dot(actives[0], weight_buf[4], preferred_element_type=jnp.float32)
    weight_copies[5].wait()
    total = total + jnp.dot(actives[1], weight_buf[5], preferred_element_type=jnp.float32)
    for i in range(pieces):
        outs[i][...] = total[i * count : (i + 1) * count].astype(outs[i].dtype)


def mlp(pieces, index, gate, up, down, near):
    count, width = pieces[0].shape
    hidden_units = gate.shape[1]
    anywhere = pl.BlockSpec(memory_space=pl.ANY)
    out = jax.ShapeDtypeStruct((count, width), jnp.bfloat16)
    return pl.pallas_call(
        lambda *refs: mlp_kernel(index, len(pieces), *refs),
        in_specs=[anywhere] * (len(pieces) + 4),
        out_shape=tuple(out for _ in pieces),
        scratch_shapes=[
            pltpu.VMEM((len(pieces) * count, width), jnp.bfloat16),
            pltpu.VMEM((6, hidden_units, width), jnp.bfloat16),
            pltpu.SemaphoreType.DMA((len(pieces),)),
            pltpu.SemaphoreType.DMA((6,)),
        ],
        name="mlp",
    )(*pieces, gate, up, down, near)


def pack_kernel(index, gate, up, down, out_ref, sem):
    parts = 4
    block = gate.shape[1] // parts
    copies = []
    for i, source in enumerate((gate, up, down)):
        for j in range(parts):
            cut = pl.ds(j * block, block)
            copies.append(
                pltpu.make_async_copy(
                    source.at[index, cut], out_ref.at[i, cut], sem.at[i * parts + j]
                )
            )
    for copy in copies:
        copy.start()
    for copy in copies:
        copy.wait()


def pack(index, gate, up, down):
    anywhere = pl.BlockSpec(memory_space=pl.ANY)
    return pl.pallas_call(
        lambda *refs: pack_kernel(index, *refs),
        in_specs=[anywhere] * 3,
        out_specs=anywhere,
        out_shape=jax.ShapeDtypeStruct((3, *gate.shape[1:]), gate.dtype),
        scratch_shapes=[pltpu.SemaphoreType.DMA((12,))],
        name="pack",
    )(gate, up, down)


def hop(sizes, move):
    count_y, count_z, count_x = sizes

    def index(y, c, z, x):
        return (
            ((y % count_y) * 2 + c) * (count_z * count_x)
            + (z % count_z) * count_x
            + x % count_x
        )

    return [
        (index(y, c, z, x), index(*move(y, c, z, x)))
        for y in range(count_y)
        for c in range(2)
        for z in range(count_z)
        for x in range(count_x)
    ]


def block(
    query_key_value, residual, norm_gain, expert_ids, route_gates, slot_index, w_gate, w_up, w_down
):
    frames_local, sites_local, model_width = residual.shape
    groups = lax.axis_size("ep")
    halves = 2
    site_groups = sites_local // SITE_GROUP
    assert site_groups * halves == groups
    half = model_width // halves
    tokens = frames_local * sites_local
    experts_local = w_gate.shape[0]
    experts_all = experts_local * groups
    capacity = 2 * tokens // experts_all
    bf16 = jnp.bfloat16

    spread = query_key_value.reshape(
        frames_local, site_groups, SITE_GROUP, 3, halves, half
    ).transpose(1, 4, 3, 0, 2, 5)
    spread = spread.reshape(groups, 3, frames_local, SITE_GROUP, half)
    gate = w_gate.transpose(0, 2, 1)
    up = w_up.transpose(0, 2, 1)
    together = lax.all_to_all(spread, "ep", split_axis=0, concat_axis=0, tiled=True)
    mixed = pl.pallas_call(
        attend_kernel,
        out_shape=jax.ShapeDtypeStruct((groups, frames_local, SITE_GROUP, half), bf16),
        name="attend",
    )(together)
    attended = lax.all_to_all(mixed, "ep", split_axis=0, concat_axis=0, tiled=True)

    sizes = (groups // 2, SIDE, lax.axis_size("tp") // SIDE)

    def along_x(steps):
        return hop(sizes, lambda y, c, z, x: (y, c, z, x + steps))

    def along_z(steps):
        return hop(sizes, lambda y, c, z, x: (y, c, z + steps, x))

    def send(value, pairs):
        return lax.ppermute(value, ("ep", "tp"), pairs)

    packed_a = pack(0, gate, up, w_down)
    packed_b = pack(1, gate, up, w_down)
    near_a = send(packed_a, hop(sizes, lambda y, c, z, x: (y, c, z, x - 1 + 2 * c)))
    near_b = send(packed_b, hop(sizes, lambda y, c, z, x: (y, c, z - 1 + 2 * c, x)))
    near = [near_a, near_b]

    target = jnp.where(slot_index >= 0, expert_ids * capacity + slot_index, -1)
    target = target.reshape(tokens, 2)
    gates = route_gates.reshape(tokens, 2)
    slots = experts_all * capacity
    hidden, rows = pl.pallas_call(
        route_kernel,
        out_shape=(
            jax.ShapeDtypeStruct((tokens, model_width), jnp.float32),
            jax.ShapeDtypeStruct((slots, model_width), bf16),
        ),
        name="route",
    )(attended, residual, norm_gain.reshape(1, model_width), target.T)
    arrived = lax.all_to_all(
        rows.reshape(groups, experts_local, capacity, model_width),
        "ep",
        split_axis=0,
        concat_axis=0,
        tiled=True,
    )
    part_rows = groups * capacity
    mine = [arrived[:, e].reshape(part_rows, model_width) for e in range(2)]
    far = (along_x, along_z)
    ring = (along_z, along_x)
    here = []
    for e in range(2):
        here.append(jnp.concatenate([mine[e], send(mine[e], far[e](2))]))

    def send_all(values, steps):
        out = []
        for e in range(2):
            out.append(send(values[e], ring[e](steps)))
        return out

    def run(e, pieces):
        return mlp(pieces, e, gate, up, w_down, near[e])

    ahead = send_all(here, 1)
    behind = send_all(here, -1)
    parts = [list(run(e, [here[e]])) for e in range(2)]
    parts, ahead, behind = lax.optimization_barrier((parts, ahead, behind))
    from_ahead = send_all([rows_in[:part_rows] for rows_in in ahead], 1)
    from_behind = send_all([rows_in[part_rows:] for rows_in in behind], -1)
    across = [jnp.concatenate([from_ahead[e], from_behind[e]]) for e in range(2)]
    done = parts
    for e in range(2):
        rows_in, done = lax.optimization_barrier(([ahead[e], behind[e]], done))
        done = run(e, rows_in)
        for part, steps in ((done[0], -1), (done[1], 1)):
            parts[e].append(send(part, ring[e](steps)))
    for e in range(2):
        rows_in, done = lax.optimization_barrier((across[e], done))
        done = run(e, [rows_in])
        parts[e].append(send(done[0], ring[e](2)))

    def add(pieces):
        total = pieces[0].astype(jnp.float32)
        for piece in pieces[1:]:
            total = total + piece.astype(jnp.float32)
        return total.astype(bf16)

    summed = []
    for e in range(2):
        opposite = add([part[part_rows:] for part in parts[e]])
        summed.append(add([part[:part_rows] for part in parts[e]] + [send(opposite, far[e](2))]))
    ready = jnp.stack([part.reshape(groups, capacity, model_width) for part in summed], axis=1)
    back = lax.all_to_all(ready, "ep", split_axis=0, concat_axis=0, tiled=True)
    combined = pl.pallas_call(
        combine_kernel,
        out_shape=jax.ShapeDtypeStruct((tokens, model_width), bf16),
        name="combine",
    )(hidden, back.reshape(slots, model_width), target, gates)
    return combined.reshape(frames_local, sites_local, model_width)


def solution(mesh):
    return jax.shard_map(
        block,
        mesh=mesh,
        in_specs=(
            P("ep", "tp", None, None),
            P("ep", "tp", None),
            P(),
            P("ep", "tp", None),
            P("ep", "tp", None),
            P("ep", "tp", None),
            P("ep", None, "tp"),
            P("ep", None, "tp"),
            P("ep", "tp", None),
        ),
        out_specs=P("ep", "tp", None),
        check_vma=False,
    )
```

```python
import math

import jax
import jax.numpy as jnp
from jax import lax
from jax.experimental import pallas as pl
from jax.experimental.pallas import tpu as pltpu
from jax.sharding import PartitionSpec as P


HD = 64
SITE_GROUP = 8
LANES = 2 * HD
SIDE = 4


def nt_dot(left, right):
    return lax.dot_general(
        left, right, (((1,), (1,)), ((), ())), preferred_element_type=jnp.float32
    )


def attend_kernel(qkv_ref, out_ref):
    sources, _, frames, sites, width = qkv_ref.shape
    rows = sources * frames * sites
    row_site = lax.broadcasted_iota(jnp.int32, (2 * rows, rows), 0) % sites
    col_site = lax.broadcasted_iota(jnp.int32, (2 * rows, rows), 1) % sites
    same_site = row_site == col_site
    low_head = lax.broadcasted_iota(jnp.int32, (rows, LANES), 1) < HD
    for pair in range(width // LANES):
        cols = pl.ds(pair * LANES, LANES)
        query = qkv_ref[:, 0, :, :, cols].reshape(rows, LANES)
        key = qkv_ref[:, 1, :, :, cols].reshape(rows, LANES)
        value = qkv_ref[:, 2, :, :, cols].reshape(rows, LANES)
        zero = jnp.zeros_like(query)
        both = jnp.concatenate(
            [jnp.where(low_head, query, zero), jnp.where(low_head, zero, query)], axis=0
        )
        scores = nt_dot(both, key) * (1.0 / math.sqrt(HD))
        scores = jnp.where(same_site, scores, -jnp.inf)
        expo = jnp.exp(scores - jnp.max(scores, axis=-1, keepdims=True))
        probs = (expo / jnp.sum(expo, axis=-1, keepdims=True)).astype(jnp.bfloat16)
        mixed = jnp.dot(probs, value, preferred_element_type=jnp.float32)
        mixed = jnp.where(low_head, mixed[:rows], mixed[rows:])
        out_ref[:, :, :, cols] = mixed.astype(out_ref.dtype).reshape(
            sources, frames, sites, LANES
        )


def route_kernel(att_ref, res_ref, gain_ref, target_ref, hidden_ref, rows_ref):
    _, frames, sites, half = att_ref.shape
    groups = att_ref.shape[0] // 2
    tokens = frames * groups * sites
    attended = jnp.concatenate(
        [
            jnp.concatenate(
                [
                    att_ref[2 * group + side, frame].astype(jnp.float32)
                    for frame in range(frames)
                    for group in range(groups)
                ],
                axis=0,
            )
            for side in range(2)
        ],
        axis=1,
    )
    hidden = res_ref[...].reshape(tokens, 2 * half).astype(jnp.float32) + attended
    hidden_ref[...] = hidden
    scale = lax.rsqrt(jnp.mean(hidden * hidden, axis=-1, keepdims=True) + 1e-06)
    normed = (hidden * scale * gain_ref[...]).astype(jnp.bfloat16)
    row = lax.broadcasted_iota(jnp.int32, (rows_ref.shape[0], tokens), 0)
    hit = (row == target_ref[0:1, :]) | (row == target_ref[1:2, :])
    picker = jnp.where(hit, 1.0, 0.0).astype(jnp.bfloat16)
    rows_ref[...] = jnp.dot(picker, normed, preferred_element_type=jnp.float32).astype(
        jnp.bfloat16
    )


def combine_kernel(hidden_ref, rows_ref, target_ref, gate_ref, out_ref):
    tokens = hidden_ref.shape[0]
    returned = rows_ref[...]
    col = lax.broadcasted_iota(jnp.int32, (tokens, returned.shape[0]), 1)
    moved = jnp.zeros(hidden_ref.shape, jnp.float32)
    for choice in range(2):
        target = target_ref[:, choice : choice + 1]
        picker = jnp.where(col == target, 1.0, 0.0).astype(jnp.bfloat16)
        weight = jnp.where(target >= 0, gate_ref[:, choice : choice + 1], 0.0)
        moved = moved + weight * jnp.dot(picker, returned, preferred_element_type=jnp.float32)
    out_ref[...] = (hidden_ref[...] + moved).astype(out_ref.dtype)


def mlp_kernel(index, pieces, *refs):
    gate, up, down, near = refs[pieces : pieces + 4]
    out = refs[pieces + 4]
    rows = [ref[...] for ref in refs[:pieces]]
    rows = rows[0] if pieces == 1 else jnp.concatenate(rows, axis=0)
    total = None
    for gate_w, up_w, down_w in (
        (gate.at[index], up.at[index], down.at[index]),
        (near.at[0], near.at[1], near.at[2]),
    ):
        gate_val = nt_dot(rows, gate_w[...])
        up_val = nt_dot(rows, up_w[...])
        active = (gate_val / (1.0 + jnp.exp(-gate_val)) * up_val).astype(jnp.bfloat16)
        part = jnp.dot(active, down_w[...], preferred_element_type=jnp.float32)
        total = part if total is None else total + part
    out[...] = total.astype(out.dtype)


def on_chip(count):
    return [pl.BlockSpec(memory_space=pltpu.VMEM)] * count


def grant(mebibytes):
    return pltpu.CompilerParams(vmem_limit_bytes=mebibytes << 20)


def mlp(pieces, index, gate, up, down, near):
    count = sum(piece.shape[0] for piece in pieces)
    return pl.pallas_call(
        lambda *refs: mlp_kernel(index, len(pieces), *refs),
        in_specs=on_chip(len(pieces) + 4),
        out_specs=on_chip(1)[0],
        out_shape=jax.ShapeDtypeStruct((count, pieces[0].shape[1]), jnp.bfloat16),
        compiler_params=grant(24),
        name="mlp",
    )(*pieces, gate, up, down, near)


def pack_kernel(index, gate, up, down, out_ref):
    for i, source in enumerate((gate, up, down)):
        out_ref[i] = source[index]


def pack(index, gate, up, down):
    return pl.pallas_call(
        lambda *refs: pack_kernel(index, *refs),
        in_specs=on_chip(3),
        out_specs=on_chip(1)[0],
        out_shape=jax.ShapeDtypeStruct((3, *gate.shape[1:]), gate.dtype),
        compiler_params=grant(18),
        name="pack",
    )(gate, up, down)


def land_kernel(source, out_ref, sem):
    copies = [
        pltpu.make_async_copy(source.at[i], out_ref.at[i], sem.at[i])
        for i in range(source.shape[0])
    ]
    for copy in copies:
        copy.start()
    for copy in copies:
        copy.wait()


def land(value):
    return pl.pallas_call(
        land_kernel,
        in_specs=[pl.BlockSpec(memory_space=pl.ANY)],
        out_specs=on_chip(1)[0],
        out_shape=pltpu.VMEM(value.shape, value.dtype),
        scratch_shapes=[pltpu.SemaphoreType.DMA((value.shape[0],))],
        compiler_params=grant(1),
        name="land",
    )(value)


def hop(sizes, move):
    count_y, count_z, count_x = sizes

    def index(y, c, z, x):
        return (
            ((y % count_y) * 2 + c) * (count_z * count_x)
            + (z % count_z) * count_x
            + x % count_x
        )

    return [
        (index(y, c, z, x), index(*move(y, c, z, x)))
        for y in range(count_y)
        for c in range(2)
        for z in range(count_z)
        for x in range(count_x)
    ]


def block(
    query_key_value, residual, norm_gain, expert_ids, route_gates, slot_index, w_gate, w_up, w_down
):
    frames_local, sites_local, model_width = residual.shape
    groups = lax.axis_size("ep")
    halves = 2
    site_groups = sites_local // SITE_GROUP
    assert site_groups * halves == groups
    half = model_width // halves
    tokens = frames_local * sites_local
    experts_local = w_gate.shape[0]
    experts_all = experts_local * groups
    capacity = 2 * tokens // experts_all
    bf16 = jnp.bfloat16

    spread = query_key_value.reshape(
        frames_local, site_groups, SITE_GROUP, 3, halves, half
    ).transpose(1, 4, 3, 0, 2, 5)
    spread = spread.reshape(groups, 3, frames_local, SITE_GROUP, half)
    gate = w_gate.transpose(0, 2, 1)
    up = w_up.transpose(0, 2, 1)
    together = lax.all_to_all(spread, "ep", split_axis=0, concat_axis=0, tiled=True)
    mixed = pl.pallas_call(
        attend_kernel,
        out_shape=jax.ShapeDtypeStruct((groups, frames_local, SITE_GROUP, half), bf16),
        in_specs=on_chip(1),
        out_specs=on_chip(1)[0],
        compiler_params=grant(16),
        name="attend",
    )(together)
    attended = lax.all_to_all(mixed, "ep", split_axis=0, concat_axis=0, tiled=True)

    sizes = (groups // 2, SIDE, lax.axis_size("tp") // SIDE)

    def along_x(steps):
        return hop(sizes, lambda y, c, z, x: (y, c, z, x + steps))

    def along_z(steps):
        return hop(sizes, lambda y, c, z, x: (y, c, z + steps, x))

    def send(value, pairs):
        return lax.ppermute(value, ("ep", "tp"), pairs)

    packed_a = pack(0, gate, up, w_down)
    packed_b = pack(1, gate, up, w_down)
    near_a = send(packed_a, hop(sizes, lambda y, c, z, x: (y, c, z, x - 1 + 2 * c)))
    near_b = send(packed_b, hop(sizes, lambda y, c, z, x: (y, c, z - 1 + 2 * c, x)))
    near = []
    for value in (near_a, near_b):
        near.append(land(value))

    target = jnp.where(slot_index >= 0, expert_ids * capacity + slot_index, -1)
    target = target.reshape(tokens, 2)
    gates = route_gates.reshape(tokens, 2)
    slots = experts_all * capacity
    hidden, rows = pl.pallas_call(
        route_kernel,
        out_shape=(
            jax.ShapeDtypeStruct((tokens, model_width), jnp.float32),
            jax.ShapeDtypeStruct((slots, model_width), bf16),
        ),
        in_specs=on_chip(4),
        out_specs=tuple(on_chip(2)),
        compiler_params=grant(12),
        name="route",
    )(attended, residual, norm_gain.reshape(1, model_width), target.T)
    arrived = lax.all_to_all(
        rows.reshape(groups, experts_local, capacity, model_width),
        "ep",
        split_axis=0,
        concat_axis=0,
        tiled=True,
    )
    part_rows = groups * capacity
    mine = [arrived[:, e].reshape(part_rows, model_width) for e in range(2)]
    far = (along_x, along_z)
    ring = (along_z, along_x)
    here = []
    for e in range(2):
        here.append(jnp.concatenate([mine[e], send(mine[e], far[e](2))]))

    def send_all(values, steps):
        out = []
        for e in range(2):
            out.append(send(values[e], ring[e](steps)))
        return out

    def run(e, pieces):
        return mlp(pieces, e, gate, up, w_down, near[e])

    ahead = send_all(here, 1)
    behind = send_all(here, -1)
    done = [run(e, [here[e]]) for e in range(2)]
    parts = [[part] for part in done]
    from_ahead, from_behind = [None, None], [None, None]
    for arrived_rows, relayed, cut, steps in (
        (ahead, from_ahead, slice(0, part_rows), 1),
        (behind, from_behind, slice(part_rows, 2 * part_rows), -1),
    ):
        for e in range(2):
            rows_in, done = lax.optimization_barrier((arrived_rows[e], done))
            relayed[e] = send(rows_in[cut], ring[e](steps))
            done = run(e, [rows_in])
            parts[e].append(send(done, ring[e](-steps)))
    for e in range(2):
        rows_in, done = lax.optimization_barrier(([from_ahead[e], from_behind[e]], done))
        done = run(e, rows_in)
        parts[e].append(send(done, ring[e](2)))

    def add(pieces):
        total = pieces[0].astype(jnp.float32)
        for piece in pieces[1:]:
            total = total + piece.astype(jnp.float32)
        return total.astype(bf16)

    summed = []
    for e in range(2):
        opposite = add([part[part_rows:] for part in parts[e]])
        summed.append(add([part[:part_rows] for part in parts[e]] + [send(opposite, far[e](2))]))
    ready = jnp.stack([part.reshape(groups, capacity, model_width) for part in summed], axis=1)
    back = lax.all_to_all(ready, "ep", split_axis=0, concat_axis=0, tiled=True)
    combined = pl.pallas_call(
        combine_kernel,
        out_shape=jax.ShapeDtypeStruct((tokens, model_width), bf16),
        in_specs=on_chip(4),
        out_specs=on_chip(1)[0],
        compiler_params=grant(12),
        name="combine",
    )(hidden, back.reshape(slots, model_width), target, gates)
    return combined.reshape(frames_local, sites_local, model_width)


def solution(mesh):
    return jax.shard_map(
        block,
        mesh=mesh,
        in_specs=(
            P("ep", "tp", None, None),
            P("ep", "tp", None),
            P(),
            P("ep", "tp", None),
            P("ep", "tp", None),
            P("ep", "tp", None),
            P("ep", None, "tp"),
            P("ep", None, "tp"),
            P("ep", "tp", None),
        ),
        out_specs=P("ep", "tp", None),
        check_vma=False,
    )
```

```python
import math

import jax
import jax.numpy as jnp
from jax import lax
from jax.experimental import pallas as pl
from jax.experimental.pallas import tpu as pltpu
from jax.sharding import PartitionSpec as P


HD = 64
SITE_GROUP = 8
LANES = 2 * HD
SIDE = 4


def nt_dot(left, right):
    return lax.dot_general(
        left, right, (((1,), (1,)), ((), ())), preferred_element_type=jnp.float32
    )


def attend_kernel(qkv_ref, out_ref):
    sources, _, frames, sites, width = qkv_ref.shape
    rows = sources * frames * sites
    row_site = lax.broadcasted_iota(jnp.int32, (2 * rows, rows), 0) % sites
    col_site = lax.broadcasted_iota(jnp.int32, (2 * rows, rows), 1) % sites
    same_site = row_site == col_site
    low_head = lax.broadcasted_iota(jnp.int32, (rows, LANES), 1) < HD
    for pair in range(width // LANES):
        cols = pl.ds(pair * LANES, LANES)
        query = qkv_ref[:, 0, :, :, cols].reshape(rows, LANES)
        key = qkv_ref[:, 1, :, :, cols].reshape(rows, LANES)
        value = qkv_ref[:, 2, :, :, cols].reshape(rows, LANES)
        zero = jnp.zeros_like(query)
        both = jnp.concatenate(
            [jnp.where(low_head, query, zero), jnp.where(low_head, zero, query)], axis=0
        )
        scores = nt_dot(both, key) * (1.0 / math.sqrt(HD))
        scores = jnp.where(same_site, scores, -jnp.inf)
        expo = jnp.exp(scores - jnp.max(scores, axis=-1, keepdims=True))
        probs = (expo / jnp.sum(expo, axis=-1, keepdims=True)).astype(jnp.bfloat16)
        mixed = jnp.dot(probs, value, preferred_element_type=jnp.float32)
        mixed = jnp.where(low_head, mixed[:rows], mixed[rows:])
        out_ref[:, :, :, cols] = mixed.astype(out_ref.dtype).reshape(
            sources, frames, sites, LANES
        )


def route_kernel(att_ref, res_ref, gain_ref, target_ref, hidden_ref, rows_ref):
    _, frames, sites, half = att_ref.shape
    groups = att_ref.shape[0] // 2
    tokens = frames * groups * sites
    attended = jnp.concatenate(
        [
            jnp.concatenate(
                [
                    att_ref[2 * group + side, frame].astype(jnp.float32)
                    for frame in range(frames)
                    for group in range(groups)
                ],
                axis=0,
            )
            for side in range(2)
        ],
        axis=1,
    )
    hidden = res_ref[...].reshape(tokens, 2 * half).astype(jnp.float32) + attended
    hidden_ref[...] = hidden
    scale = lax.rsqrt(jnp.mean(hidden * hidden, axis=-1, keepdims=True) + 1e-06)
    normed = (hidden * scale * gain_ref[...]).astype(jnp.bfloat16)
    row = lax.broadcasted_iota(jnp.int32, (rows_ref.shape[0], tokens), 0)
    hit = (row == target_ref[0:1, :]) | (row == target_ref[1:2, :])
    picker = jnp.where(hit, 1.0, 0.0).astype(jnp.bfloat16)
    rows_ref[...] = jnp.dot(picker, normed, preferred_element_type=jnp.float32).astype(
        jnp.bfloat16
    )


def combine_kernel(hidden_ref, rows_ref, target_ref, gate_ref, out_ref):
    tokens = hidden_ref.shape[0]
    returned = rows_ref[...]
    col = lax.broadcasted_iota(jnp.int32, (tokens, returned.shape[0]), 1)
    moved = jnp.zeros(hidden_ref.shape, jnp.float32)
    for choice in range(2):
        target = target_ref[:, choice : choice + 1]
        picker = jnp.where(col == target, 1.0, 0.0).astype(jnp.bfloat16)
        weight = jnp.where(target >= 0, gate_ref[:, choice : choice + 1], 0.0)
        moved = moved + weight * jnp.dot(picker, returned, preferred_element_type=jnp.float32)
    out_ref[...] = (hidden_ref[...] + moved).astype(out_ref.dtype)


def mlp_kernel(index, pieces, *refs):
    gate, up, down, near, out = refs[pieces:]
    rows = [ref[...] for ref in refs[:pieces]]
    rows = rows[0] if pieces == 1 else jnp.concatenate(rows, axis=0)
    total = None
    for gate_w, up_w, down_w in (
        (gate.at[index], up.at[index], down.at[index]),
        (near.at[0], near.at[1], near.at[2]),
    ):
        gate_val = nt_dot(rows, gate_w[...])
        up_val = nt_dot(rows, up_w[...])
        active = (gate_val / (1.0 + jnp.exp(-gate_val)) * up_val).astype(jnp.bfloat16)
        part = jnp.dot(active, down_w[...], preferred_element_type=jnp.float32)
        total = part if total is None else total + part
    out[...] = total.astype(out.dtype)


def on_chip(count):
    return [pl.BlockSpec(memory_space=pltpu.VMEM)] * count


def grant(mebibytes):
    return pltpu.CompilerParams(vmem_limit_bytes=mebibytes << 20)


def mlp(pieces, index, gate, up, down, near):
    count = sum(piece.shape[0] for piece in pieces)
    return pl.pallas_call(
        lambda *refs: mlp_kernel(index, len(pieces), *refs),
        in_specs=on_chip(len(pieces) + 4),
        out_specs=on_chip(1)[0],
        out_shape=jax.ShapeDtypeStruct((count, pieces[0].shape[1]), jnp.bfloat16),
        compiler_params=grant(24),
        name="mlp",
    )(*pieces, gate, up, down, near)


def pack_kernel(gate, up, down, out_ref):
    for i, source in enumerate((gate, up, down)):
        out_ref[i] = source[...]


def pack(index, gate, up, down):
    steps = 4
    _, rows, width = gate.shape
    return pl.pallas_call(
        pack_kernel,
        grid=(steps,),
        in_specs=[pl.BlockSpec((None, rows // steps, width), lambda i: (index, i, 0))] * 3,
        out_specs=pl.BlockSpec((3, rows // steps, width), lambda i: (0, i, 0)),
        out_shape=jax.ShapeDtypeStruct((3, rows, width), gate.dtype),
        compiler_params=grant(58),
        name="pack",
    )(gate, up, down)


def land_kernel(source, out_ref, sem):
    copies = [
        pltpu.make_async_copy(source.at[i], out_ref.at[i], sem.at[i])
        for i in range(source.shape[0])
    ]
    for copy in copies:
        copy.start()
    for copy in copies:
        copy.wait()


def land(value):
    return pl.pallas_call(
        land_kernel,
        in_specs=[pl.BlockSpec(memory_space=pltpu.HBM)],
        out_specs=on_chip(1)[0],
        out_shape=pltpu.VMEM(value.shape, value.dtype),
        scratch_shapes=[pltpu.SemaphoreType.DMA((value.shape[0],))],
        compiler_params=grant(6),
        name="land",
    )(value)


def hop(sizes, move):
    count_y, count_z, count_x = sizes

    def index(y, c, z, x):
        return (
            ((y % count_y) * 2 + c) * (count_z * count_x)
            + (z % count_z) * count_x
            + x % count_x
        )

    return [
        (index(y, c, z, x), index(*move(y, c, z, x)))
        for y in range(count_y)
        for c in range(2)
        for z in range(count_z)
        for x in range(count_x)
    ]


def block(
    query_key_value, residual, norm_gain, expert_ids, route_gates, slot_index, w_gate, w_up, w_down
):
    frames_local, sites_local, model_width = residual.shape
    groups = lax.axis_size("ep")
    halves = 2
    site_groups = sites_local // SITE_GROUP
    assert site_groups * halves == groups
    half = model_width // halves
    tokens = frames_local * sites_local
    experts_local = w_gate.shape[0]
    experts_all = experts_local * groups
    capacity = 2 * tokens // experts_all
    bf16 = jnp.bfloat16

    spread = query_key_value.reshape(
        frames_local, site_groups, SITE_GROUP, 3, halves, half
    ).transpose(1, 4, 3, 0, 2, 5)
    spread = spread.reshape(groups, 3, frames_local, SITE_GROUP, half)
    gate = w_gate.transpose(0, 2, 1)
    up = w_up.transpose(0, 2, 1)
    together = lax.all_to_all(spread, "ep", split_axis=0, concat_axis=0, tiled=True)
    mixed = pl.pallas_call(
        attend_kernel,
        out_shape=jax.ShapeDtypeStruct((groups, frames_local, SITE_GROUP, half), bf16),
        in_specs=on_chip(1),
        compiler_params=grant(16),
        name="attend",
    )(together)
    attended = lax.all_to_all(mixed, "ep", split_axis=0, concat_axis=0, tiled=True)

    sizes = (groups // 2, SIDE, lax.axis_size("tp") // SIDE)

    def along_x(steps):
        return hop(sizes, lambda y, c, z, x: (y, c, z, x + steps))

    def along_z(steps):
        return hop(sizes, lambda y, c, z, x: (y, c, z + steps, x))

    def send(value, pairs):
        return lax.ppermute(value, ("ep", "tp"), pairs)

    packed_a = pack(0, gate, up, w_down)
    packed_b = pack(1, gate, up, w_down)
    near_a = send(packed_a, hop(sizes, lambda y, c, z, x: (y, c, z, x - 1 + 2 * c)))
    near_b = send(packed_b, hop(sizes, lambda y, c, z, x: (y, c, z - 1 + 2 * c, x)))
    near = []
    for value in (near_a, near_b):
        near.append(land(value))

    target = jnp.where(slot_index >= 0, expert_ids * capacity + slot_index, -1)
    target = target.reshape(tokens, 2)
    gates = route_gates.reshape(tokens, 2)
    slots = experts_all * capacity
    hidden, rows = pl.pallas_call(
        route_kernel,
        out_shape=(
            jax.ShapeDtypeStruct((tokens, model_width), jnp.float32),
            jax.ShapeDtypeStruct((slots, model_width), bf16),
        ),
        in_specs=on_chip(1) + [pl.BlockSpec()] + on_chip(2),
        out_specs=(pl.BlockSpec(), on_chip(1)[0]),
        compiler_params=grant(12),
        name="route",
    )(attended, residual, norm_gain.reshape(1, model_width), target.T)
    arrived = lax.all_to_all(
        rows.reshape(groups, experts_local, capacity, model_width),
        "ep",
        split_axis=0,
        concat_axis=0,
        tiled=True,
    )
    part_rows = groups * capacity
    mine = [arrived[:, e].reshape(part_rows, model_width) for e in range(2)]
    far = (along_x, along_z)
    ring = (along_z, along_x)

    def send_all(values, moves, steps):
        out = []
        for e in range(2):
            out.append(send(values[e], moves[e](steps)))
        return out

    def run(e, pieces, after):
        pieces, _ = lax.optimization_barrier((pieces, after))
        return mlp(pieces, e, gate, up, w_down, near[e])

    other = send_all(mine, far, 2)
    ahead = [send_all(mine, ring, 1)]
    behind = [send_all(mine, ring, -1)]
    ahead.append(send_all(other, ring, 1))
    behind.append(send_all(other, ring, -1))
    across = [send_all(ahead[0], ring, 1), send_all(behind[1], ring, -1)]
    done = ()
    parts = []
    for e in range(2):
        done = run(e, [mine[e], other[e]], done)
        parts.append([done])
    for pieces, steps in ((ahead, -1), (behind, 1), (across, 2)):
        for e in range(2):
            done = run(e, [pieces[0][e], pieces[1][e]], done)
            parts[e].append(send(done, ring[e](steps)))

    def add(pieces):
        total = pieces[0].astype(jnp.float32)
        for piece in pieces[1:]:
            total = total + piece.astype(jnp.float32)
        return total.astype(bf16)

    summed = []
    for e in range(2):
        opposite = add([part[part_rows:] for part in parts[e]])
        summed.append(add([part[:part_rows] for part in parts[e]] + [send(opposite, far[e](2))]))
    ready = jnp.stack([part.reshape(groups, capacity, model_width) for part in summed], axis=1)
    back = lax.all_to_all(ready, "ep", split_axis=0, concat_axis=0, tiled=True)
    combined = pl.pallas_call(
        combine_kernel,
        out_shape=jax.ShapeDtypeStruct((tokens, model_width), bf16),
        in_specs=on_chip(4),
        compiler_params=grant(12),
        name="combine",
    )(hidden, back.reshape(slots, model_width), target, gates)
    return combined.reshape(frames_local, sites_local, model_width)


def solution(mesh):
    return jax.shard_map(
        block,
        mesh=mesh,
        in_specs=(
            P("ep", "tp", None, None),
            P("ep", "tp", None),
            P(),
            P("ep", "tp", None),
            P("ep", "tp", None),
            P("ep", "tp", None),
            P("ep", None, "tp"),
            P("ep", None, "tp"),
            P("ep", "tp", None),
        ),
        out_specs=P("ep", "tp", None),
        check_vma=False,
    )
```

```python
import math

import jax
import jax.numpy as jnp
from jax import lax
from jax.experimental import pallas as pl
from jax.experimental.pallas import tpu as pltpu
from jax.sharding import PartitionSpec as P


HD = 64
SITE_GROUP = 8
LANES = 2 * HD
SIDE = 4


def nt_dot(left, right):
    return lax.dot_general(
        left, right, (((1,), (1,)), ((), ())), preferred_element_type=jnp.float32
    )


def attend_kernel(qkv_ref, out_ref):
    sources, _, frames, sites, width = qkv_ref.shape
    rows = sources * frames * sites
    row_site = lax.broadcasted_iota(jnp.int32, (2 * rows, rows), 0) % sites
    col_site = lax.broadcasted_iota(jnp.int32, (2 * rows, rows), 1) % sites
    same_site = row_site == col_site
    low_head = lax.broadcasted_iota(jnp.int32, (rows, LANES), 1) < HD

    @pl.loop(0, width // LANES)
    def _(pair):
        cols = pl.ds(pl.multiple_of(pair * LANES, LANES), LANES)
        query = qkv_ref[:, 0, :, :, cols].reshape(rows, LANES)
        key = qkv_ref[:, 1, :, :, cols].reshape(rows, LANES)
        value = qkv_ref[:, 2, :, :, cols].reshape(rows, LANES)
        zero = jnp.zeros_like(query)
        both = jnp.concatenate(
            [jnp.where(low_head, query, zero), jnp.where(low_head, zero, query)], axis=0
        )
        scores = nt_dot(both, key) * (1.0 / math.sqrt(HD))
        scores = jnp.where(same_site, scores, -jnp.inf)
        expo = jnp.exp(scores - jnp.max(scores, axis=-1, keepdims=True))
        probs = (expo / jnp.sum(expo, axis=-1, keepdims=True)).astype(jnp.bfloat16)
        mixed = jnp.dot(probs, value, preferred_element_type=jnp.float32)
        mixed = jnp.where(low_head, mixed[:rows], mixed[rows:])
        out_ref[:, :, :, cols] = mixed.astype(out_ref.dtype).reshape(
            sources, frames, sites, LANES
        )


def route_kernel(att_ref, res_ref, gain_ref, target_ref, hidden_ref, rows_ref):
    _, frames, sites, half = att_ref.shape
    groups = att_ref.shape[0] // 2
    tokens = frames * groups * sites
    attended = jnp.concatenate(
        [
            jnp.concatenate(
                [
                    att_ref[2 * group + side, frame].astype(jnp.float32)
                    for frame in range(frames)
                    for group in range(groups)
                ],
                axis=0,
            )
            for side in range(2)
        ],
        axis=1,
    )
    hidden = res_ref[...].reshape(tokens, 2 * half).astype(jnp.float32) + attended
    hidden_ref[...] = hidden
    scale = lax.rsqrt(jnp.mean(hidden * hidden, axis=-1, keepdims=True) + 1e-06)
    normed = (hidden * scale * gain_ref[...]).astype(jnp.bfloat16)
    row = lax.broadcasted_iota(jnp.int32, (rows_ref.shape[0], tokens), 0)
    hit = (row == target_ref[0:1, :]) | (row == target_ref[1:2, :])
    picker = jnp.where(hit, 1.0, 0.0).astype(jnp.bfloat16)
    rows_ref[...] = jnp.dot(picker, normed, preferred_element_type=jnp.float32).astype(
        jnp.bfloat16
    )


def combine_kernel(hidden_ref, rows_ref, target_ref, gate_ref, out_ref):
    tokens = hidden_ref.shape[0]
    returned = rows_ref[...]
    col = lax.broadcasted_iota(jnp.int32, (tokens, returned.shape[0]), 1)
    moved = jnp.zeros(hidden_ref.shape, jnp.float32)
    for choice in range(2):
        target = target_ref[:, choice : choice + 1]
        picker = jnp.where(col == target, 1.0, 0.0).astype(jnp.bfloat16)
        weight = jnp.where(target >= 0, gate_ref[:, choice : choice + 1], 0.0)
        moved = moved + weight * jnp.dot(picker, returned, preferred_element_type=jnp.float32)
    out_ref[...] = (hidden_ref[...] + moved).astype(out_ref.dtype)


def mlp_kernel(pieces, *refs):
    weights = refs[pieces]
    outs = refs[pieces + 1 : -1]
    total = refs[-1]
    rows = jnp.concatenate([ref[...] for ref in refs[:pieces]], axis=0)
    total[...] = jnp.zeros(total.shape, total.dtype)

    @pl.loop(0, weights.shape[0])
    def _(i):
        gate_val = nt_dot(rows, weights[i, 0])
        up_val = nt_dot(rows, weights[i, 1])
        active = (gate_val / (1.0 + jnp.exp(-gate_val)) * up_val).astype(jnp.bfloat16)
        total[...] += jnp.dot(active, weights[i, 2], preferred_element_type=jnp.float32)

    count = total.shape[0] // pieces
    for i, out in enumerate(outs):
        out[...] = total[i * count : (i + 1) * count].astype(out.dtype)


def on_chip(count):
    return [pl.BlockSpec(memory_space=pltpu.VMEM)] * count


def grant(mebibytes):
    return pltpu.CompilerParams(vmem_limit_bytes=mebibytes << 20)


def mlp(pieces, dtype, weights):
    rows = sum(piece.shape[0] for piece in pieces)
    return pl.pallas_call(
        lambda *refs: mlp_kernel(len(pieces), *refs),
        in_specs=on_chip(len(pieces) + 1),
        out_specs=tuple(on_chip(len(pieces))),
        out_shape=tuple(jax.ShapeDtypeStruct(piece.shape, dtype) for piece in pieces),
        scratch_shapes=[pltpu.VMEM((rows, pieces[0].shape[1]), jnp.float32)],
        compiler_params=grant(18),
        name="mlp",
    )(*pieces, weights)


def pack_kernel(gate, up, down, out_ref):
    for i, source in enumerate((gate, up, down)):
        out_ref[i] = source[...]


def pack(index, gate, up, down):
    steps = 4
    _, rows, width = gate.shape
    return pl.pallas_call(
        pack_kernel,
        grid=(steps,),
        in_specs=[pl.BlockSpec((None, rows // steps, width), lambda i: (index, i, 0))] * 3,
        out_specs=pl.BlockSpec((3, rows // steps, width), lambda i: (0, i, 0)),
        out_shape=jax.ShapeDtypeStruct((3, rows, width), gate.dtype),
        compiler_params=grant(58),
        name="pack",
    )(gate, up, down)


def land_kernel(own, near, out_ref, sem):
    copies = [
        pltpu.make_async_copy(near.at[i], out_ref.at[1, i], sem.at[i])
        for i in range(near.shape[0])
    ]
    for copy in copies:
        copy.start()
    out_ref[0] = own[...]
    for copy in copies:
        copy.wait()


def land(own, near):
    return pl.pallas_call(
        land_kernel,
        in_specs=on_chip(1) + [pl.BlockSpec(memory_space=pltpu.HBM)],
        out_specs=on_chip(1)[0],
        out_shape=pltpu.VMEM((2, *own.shape), own.dtype),
        scratch_shapes=[pltpu.SemaphoreType.DMA((own.shape[0],))],
        compiler_params=grant(16),
        name="land",
    )(own, near)


def hop(sizes, move):
    count_y, count_z, count_x = sizes

    def index(y, c, z, x):
        return (
            ((y % count_y) * 2 + c) * (count_z * count_x)
            + (z % count_z) * count_x
            + x % count_x
        )

    return [
        (index(y, c, z, x), index(*move(y, c, z, x)))
        for y in range(count_y)
        for c in range(2)
        for z in range(count_z)
        for x in range(count_x)
    ]


def block(
    query_key_value, residual, norm_gain, expert_ids, route_gates, slot_index, w_gate, w_up, w_down
):
    frames_local, sites_local, model_width = residual.shape
    groups = lax.axis_size("ep")
    halves = 2
    site_groups = sites_local // SITE_GROUP
    assert site_groups * halves == groups
    half = model_width // halves
    tokens = frames_local * sites_local
    experts_local = w_gate.shape[0]
    experts_all = experts_local * groups
    capacity = 2 * tokens // experts_all
    bf16 = jnp.bfloat16

    spread = query_key_value.reshape(
        frames_local, site_groups, SITE_GROUP, 3, halves, half
    ).transpose(1, 4, 3, 0, 2, 5)
    spread = spread.reshape(groups, 3, frames_local, SITE_GROUP, half)
    gate = w_gate.transpose(0, 2, 1)
    up = w_up.transpose(0, 2, 1)
    together = lax.all_to_all(spread, "ep", split_axis=0, concat_axis=0, tiled=True)
    mixed = pl.pallas_call(
        attend_kernel,
        out_shape=jax.ShapeDtypeStruct((groups, frames_local, SITE_GROUP, half), bf16),
        in_specs=on_chip(1),
        compiler_params=grant(16),
        name="attend",
    )(together)
    attended = lax.all_to_all(mixed, "ep", split_axis=0, concat_axis=0, tiled=True)

    sizes = (groups // 2, SIDE, lax.axis_size("tp") // SIDE)

    def along_x(steps):
        return hop(sizes, lambda y, c, z, x: (y, c, z, x + steps))

    def along_z(steps):
        return hop(sizes, lambda y, c, z, x: (y, c, z + steps, x))

    def send(value, pairs):
        return lax.ppermute(value, ("ep", "tp"), pairs)

    packed_a = pack(0, gate, up, w_down)
    packed_b = pack(1, gate, up, w_down)
    near_a = send(packed_a, hop(sizes, lambda y, c, z, x: (y, c, z, x - 1 + 2 * c)))
    near_b = send(packed_b, hop(sizes, lambda y, c, z, x: (y, c, z - 1 + 2 * c, x)))
    weights = []
    for own_part, near_part in ((packed_a, near_a), (packed_b, near_b)):
        weights.append(land(own_part, near_part))

    target = jnp.where(slot_index >= 0, expert_ids * capacity + slot_index, -1)
    target = target.reshape(tokens, 2)
    gates = route_gates.reshape(tokens, 2)
    slots = experts_all * capacity
    hidden, rows = pl.pallas_call(
        route_kernel,
        out_shape=(
            jax.ShapeDtypeStruct((tokens, model_width), jnp.float32),
            jax.ShapeDtypeStruct((slots, model_width), bf16),
        ),
        in_specs=on_chip(1) + [pl.BlockSpec()] + on_chip(2),
        out_specs=(pl.BlockSpec(), on_chip(1)[0]),
        compiler_params=grant(12),
        name="route",
    )(attended, residual, norm_gain.reshape(1, model_width), target.T)
    arrived = lax.all_to_all(
        rows.reshape(groups, experts_local, capacity, model_width),
        "ep",
        split_axis=0,
        concat_axis=0,
        tiled=True,
    )
    part_rows = groups * capacity
    mine = [arrived[:, e].reshape(part_rows, model_width) for e in range(2)]
    far = (along_x, along_z)
    ring = (along_z, along_x)

    def send_all(values, moves, steps):
        out = []
        for e in range(2):
            out.append(send(values[e], moves[e](steps)))
        return out

    done = ()

    def run(e, pieces, dtype=bf16):
        nonlocal done
        pieces, _ = lax.optimization_barrier((pieces, done))
        done = mlp(pieces, dtype, weights[e])
        return done

    other = send_all(mine, far, 2)
    ahead_mine = send_all(mine, ring, 1)
    behind_mine = send_all(mine, ring, -1)
    ahead_other = send_all(other, ring, 1)
    behind_other = send_all(other, ring, -1)
    cross_mine = send_all(ahead_mine, ring, 1)
    cross_other = send_all(behind_other, ring, -1)
    own = [run(e, [mine[e], other[e]]) for e in range(2)]
    first = [run(e, [ahead_mine[e], behind_other[e]]) for e in range(2)]
    first_mine = send_all([out[0] for out in first], ring, -1)
    first_other = send_all([out[1] for out in first], ring, 1)
    cross = [run(e, [cross_mine[e], cross_other[e]]) for e in range(2)]
    pass_mine = send_all([out[0] for out in cross], ring, 1)
    pass_other = send_all([out[1] for out in cross], ring, -1)
    late = [run(e, [ahead_other[e], behind_mine[e]], jnp.float32) for e in range(2)]

    def add(*pieces):
        total = pieces[0].astype(jnp.float32)
        for piece in pieces[1:]:
            total = total + piece.astype(jnp.float32)
        return total.astype(bf16)

    last_other = send_all([add(late[e][0], pass_other[e]) for e in range(2)], ring, -1)
    last_mine = send_all([add(late[e][1], pass_mine[e]) for e in range(2)], ring, 1)
    swapped = send_all([add(own[e][1], first_other[e], last_other[e]) for e in range(2)], far, 2)
    summed = [
        add(own[e][0], first_mine[e], last_mine[e], swapped[e]) for e in range(2)
    ]
    ready = jnp.stack([part.reshape(groups, capacity, model_width) for part in summed], axis=1)
    back = lax.all_to_all(ready, "ep", split_axis=0, concat_axis=0, tiled=True)
    combined = pl.pallas_call(
        combine_kernel,
        out_shape=jax.ShapeDtypeStruct((tokens, model_width), bf16),
        in_specs=on_chip(4),
        compiler_params=grant(12),
        name="combine",
    )(hidden, back.reshape(slots, model_width), target, gates)
    return combined.reshape(frames_local, sites_local, model_width)


def solution(mesh):
    return jax.shard_map(
        block,
        mesh=mesh,
        in_specs=(
            P("ep", "tp", None, None),
            P("ep", "tp", None),
            P(),
            P("ep", "tp", None),
            P("ep", "tp", None),
            P("ep", "tp", None),
            P("ep", None, "tp"),
            P("ep", None, "tp"),
            P("ep", "tp", None),
        ),
        out_specs=P("ep", "tp", None),
        check_vma=False,
    )
```

```python
import math

import jax
import jax.numpy as jnp
from jax import lax
from jax.experimental import pallas as pl
from jax.experimental.pallas import tpu as pltpu
from jax.sharding import PartitionSpec as P


HD = 64
SITE_GROUP = 8
LANES = 2 * HD
SIDE = 4


def nt_dot(left, right):
    return lax.dot_general(
        left, right, (((1,), (1,)), ((), ())), preferred_element_type=jnp.float32
    )


def attend_kernel(qkv_ref, out_ref):
    sources, _, frames, sites, width = qkv_ref.shape
    rows = sources * frames * sites
    row_site = lax.broadcasted_iota(jnp.int32, (2 * rows, rows), 0) % sites
    col_site = lax.broadcasted_iota(jnp.int32, (2 * rows, rows), 1) % sites
    same_site = row_site == col_site
    low_head = lax.broadcasted_iota(jnp.int32, (rows, LANES), 1) < HD
    for pair in range(width // LANES):
        cols = pl.ds(pair * LANES, LANES)
        query = qkv_ref[:, 0, :, :, cols].reshape(rows, LANES)
        key = qkv_ref[:, 1, :, :, cols].reshape(rows, LANES)
        value = qkv_ref[:, 2, :, :, cols].reshape(rows, LANES)
        zero = jnp.zeros_like(query)
        both = jnp.concatenate(
            [jnp.where(low_head, query, zero), jnp.where(low_head, zero, query)], axis=0
        )
        scores = nt_dot(both, key) * (1.0 / math.sqrt(HD))
        scores = jnp.where(same_site, scores, -jnp.inf)
        expo = jnp.exp(scores - jnp.max(scores, axis=-1, keepdims=True))
        probs = (expo / jnp.sum(expo, axis=-1, keepdims=True)).astype(jnp.bfloat16)
        mixed = jnp.dot(probs, value, preferred_element_type=jnp.float32)
        mixed = jnp.where(low_head, mixed[:rows], mixed[rows:])
        out_ref[:, :, :, cols] = mixed.astype(out_ref.dtype).reshape(
            sources, frames, sites, LANES
        )


def route_kernel(att_ref, res_ref, gain_ref, target_ref, hidden_ref, rows_ref):
    _, frames, sites, half = att_ref.shape
    groups = att_ref.shape[0] // 2
    tokens = frames * groups * sites
    attended = jnp.concatenate(
        [
            jnp.concatenate(
                [
                    att_ref[2 * group + side, frame].astype(jnp.float32)
                    for frame in range(frames)
                    for group in range(groups)
                ],
                axis=0,
            )
            for side in range(2)
        ],
        axis=1,
    )
    hidden = res_ref[...].reshape(tokens, 2 * half).astype(jnp.float32) + attended
    hidden_ref[...] = hidden
    scale = lax.rsqrt(jnp.mean(hidden * hidden, axis=-1, keepdims=True) + 1e-06)
    normed = (hidden * scale * gain_ref[...]).astype(jnp.bfloat16)
    row = lax.broadcasted_iota(jnp.int32, (rows_ref.shape[0], tokens), 0)
    hit = (row == target_ref[0:1, :]) | (row == target_ref[1:2, :])
    picker = jnp.where(hit, 1.0, 0.0).astype(jnp.bfloat16)
    rows_ref[...] = jnp.dot(picker, normed, preferred_element_type=jnp.float32).astype(
        jnp.bfloat16
    )


def settle_kernel(position, *refs):
    own, moved, outs = refs[:2], refs[2:8], refs[8:]
    count = outs[0].shape[1]
    for k, out in enumerate(outs):
        start = pl.multiple_of((position[0] ^ k) * count, count)
        cut = pl.ds(start, count)
        for e in range(2):
            total = own[e][cut].astype(jnp.float32)
            for part in moved[3 * e : 3 * e + 3]:
                total = total + part[cut].astype(jnp.float32)
            out[e] = total.astype(out.dtype)


def combine_kernel(hidden_ref, target_ref, gate_ref, *refs):
    pieces, out_ref = refs[:-1], refs[-1]
    tokens, width = hidden_ref.shape
    returned = jnp.concatenate(
        [piece[e] for piece in pieces for e in range(piece.shape[0])], axis=0
    )
    col = lax.broadcasted_iota(jnp.int32, (tokens, returned.shape[0]), 1)
    moved = jnp.zeros((tokens, width), jnp.float32)
    for choice in range(2):
        target = target_ref[:, choice : choice + 1]
        picker = jnp.where(col == target, 1.0, 0.0).astype(jnp.bfloat16)
        weight = jnp.where(target >= 0, gate_ref[:, choice : choice + 1], 0.0)
        moved = moved + weight * jnp.dot(picker, returned, preferred_element_type=jnp.float32)
    out_ref[...] = (hidden_ref[...] + moved).astype(out_ref.dtype)


def mlp_kernel(pieces, *refs):
    weights = refs[pieces]
    outs = refs[pieces + 1 : -1]
    total = refs[-1]
    rows = jnp.concatenate([ref[...] for ref in refs[:pieces]], axis=0)
    total[...] = jnp.zeros(total.shape, total.dtype)

    @pl.loop(0, weights.shape[0])
    def _(i):
        gate_val = nt_dot(rows, weights[i, 0])
        up_val = nt_dot(rows, weights[i, 1])
        active = (gate_val / (1.0 + jnp.exp(-gate_val)) * up_val).astype(jnp.bfloat16)
        total[...] += jnp.dot(active, weights[i, 2], preferred_element_type=jnp.float32)

    count = total.shape[0] // pieces
    for i, out in enumerate(outs):
        out[...] = total[i * count : (i + 1) * count].astype(out.dtype)


def on_chip(count):
    return [pl.BlockSpec(memory_space=pltpu.VMEM)] * count


def grant(mebibytes):
    return pltpu.CompilerParams(vmem_limit_bytes=mebibytes << 20)


def mlp(pieces, dtype, weights):
    rows = sum(piece.shape[0] for piece in pieces)
    return pl.pallas_call(
        lambda *refs: mlp_kernel(len(pieces), *refs),
        in_specs=on_chip(len(pieces) + 1),
        out_specs=tuple(on_chip(len(pieces))),
        out_shape=tuple(jax.ShapeDtypeStruct(piece.shape, dtype) for piece in pieces),
        scratch_shapes=[pltpu.VMEM((rows, pieces[0].shape[1]), jnp.float32)],
        compiler_params=grant(18),
        name="mlp",
    )(*pieces, weights)


def pack_kernel(*refs):
    for i, source in enumerate(refs[:-1]):
        refs[-1][i] = source[...]


def pack(index, *sources):
    steps = 4
    _, rows, width = sources[0].shape
    count = len(sources)
    return pl.pallas_call(
        pack_kernel,
        grid=(steps,),
        in_specs=[pl.BlockSpec((None, rows // steps, width), lambda i: (index, i, 0))] * count,
        out_specs=pl.BlockSpec((count, rows // steps, width), lambda i: (0, i, 0)),
        out_shape=jax.ShapeDtypeStruct((count, rows, width), sources[0].dtype),
        compiler_params=grant(58),
        name="pack",
    )(*sources)


def land_kernel(index, gate, up, down, near_gate, near_rest, out_ref, sem):
    sources = (
        (gate.at[index], up.at[index], down.at[index]),
        (near_gate.at[0], near_rest.at[0], near_rest.at[1]),
    )
    copies = [
        pltpu.make_async_copy(source, out_ref.at[i, j], sem.at[i, j])
        for i, group in enumerate(sources)
        for j, source in enumerate(group)
    ]
    for copy in copies:
        copy.start()
    for copy in copies:
        copy.wait()


def land(index, *sources):
    held = [pltpu.with_memory_space_constraint(source, pltpu.HBM) for source in sources]
    _, rows, width = sources[0].shape
    return pl.pallas_call(
        lambda *refs: land_kernel(index, *refs),
        in_specs=[pl.BlockSpec(memory_space=pltpu.HBM)] * len(held),
        out_specs=on_chip(1)[0],
        out_shape=pltpu.VMEM((2, 3, rows, width), sources[0].dtype),
        scratch_shapes=[pltpu.SemaphoreType.DMA((2, 3))],
        compiler_params=grant(11),
        name="land",
    )(*held)


def hop(sizes, move):
    count_y, count_z, count_x = sizes

    def index(y, c, z, x):
        return (
            ((y % count_y) * 2 + c) * (count_z * count_x)
            + (z % count_z) * count_x
            + x % count_x
        )

    return [
        (index(y, c, z, x), index(*move(y, c, z, x)))
        for y in range(count_y)
        for c in range(2)
        for z in range(count_z)
        for x in range(count_x)
    ]


def block(
    query_key_value, residual, norm_gain, expert_ids, route_gates, slot_index, w_gate, w_up, w_down
):
    frames_local, sites_local, model_width = residual.shape
    groups = lax.axis_size("ep")
    halves = 2
    site_groups = sites_local // SITE_GROUP
    assert site_groups * halves == groups
    half = model_width // halves
    tokens = frames_local * sites_local
    experts_local = w_gate.shape[0]
    experts_all = experts_local * groups
    capacity = 2 * tokens // experts_all
    bf16 = jnp.bfloat16

    spread = query_key_value.reshape(
        frames_local, site_groups, SITE_GROUP, 3, halves, half
    ).transpose(1, 4, 3, 0, 2, 5)
    spread = spread.reshape(groups, 3, frames_local, SITE_GROUP, half)
    gate = w_gate.transpose(0, 2, 1)
    up = w_up.transpose(0, 2, 1)
    together = lax.all_to_all(spread, "ep", split_axis=0, concat_axis=0, tiled=True)
    mixed = pl.pallas_call(
        attend_kernel,
        out_shape=jax.ShapeDtypeStruct((groups, frames_local, SITE_GROUP, half), bf16),
        in_specs=on_chip(1),
        compiler_params=grant(16),
        name="attend",
    )(together)
    attended = lax.all_to_all(mixed, "ep", split_axis=0, concat_axis=0, tiled=True)

    sizes = (groups // 2, SIDE, lax.axis_size("tp") // SIDE)

    def along_x(steps):
        return hop(sizes, lambda y, c, z, x: (y, c, z, x + steps))

    def along_z(steps):
        return hop(sizes, lambda y, c, z, x: (y, c, z + steps, x))

    def send(value, pairs):
        return lax.ppermute(value, ("ep", "tp"), pairs)

    beside = (
        hop(sizes, lambda y, c, z, x: (y, c, z, x - 1 + 2 * c)),
        hop(sizes, lambda y, c, z, x: (y, c, z - 1 + 2 * c, x)),
    )
    near = [[], []]
    for sources in ((gate,), (up, w_down)):
        for e in range(2):
            packed = pack(e, *sources)
            near[e].append(send(packed, beside[e]))
    weights = []
    for e in range(2):
        weights.append(land(e, gate, up, w_down, *near[e]))

    target = jnp.where(slot_index >= 0, expert_ids * capacity + slot_index, -1)
    target = target.reshape(tokens, 2)
    gates = route_gates.reshape(tokens, 2)
    slots = experts_all * capacity
    hidden, rows = pl.pallas_call(
        route_kernel,
        out_shape=(
            jax.ShapeDtypeStruct((tokens, model_width), jnp.float32),
            jax.ShapeDtypeStruct((slots, model_width), bf16),
        ),
        in_specs=on_chip(1) + [pl.BlockSpec()] + on_chip(2),
        out_specs=(pl.BlockSpec(), on_chip(1)[0]),
        compiler_params=grant(12),
        name="route",
    )(attended, residual, norm_gain.reshape(1, model_width), target.T)
    arrived = lax.all_to_all(
        rows.reshape(groups, experts_local, capacity, model_width),
        "ep",
        split_axis=0,
        concat_axis=0,
        tiled=True,
    )
    part_rows = groups * capacity
    mine = [arrived[:, e].reshape(part_rows, model_width) for e in range(2)]
    far = (along_x, along_z)
    ring = (along_z, along_x)

    def send_all(values, moves, steps):
        out = []
        for e in range(2):
            out.append(send(values[e], moves[e](steps)))
        return out

    done = ()

    def run(e, pieces, dtype=bf16):
        nonlocal done
        pieces, _ = lax.optimization_barrier((pieces, done))
        done = mlp(pieces, dtype, weights[e])
        return done

    other = send_all(mine, far, 2)
    ahead_mine = send_all(mine, ring, 1)
    behind_mine = send_all(mine, ring, -1)
    ahead_other = send_all(other, ring, 1)
    behind_other = send_all(other, ring, -1)
    cross_mine = send_all(ahead_mine, ring, 1)
    cross_other = send_all(behind_other, ring, -1)
    own = [run(e, [mine[e], other[e]]) for e in range(2)]
    first = [run(e, [ahead_mine[e], behind_other[e]]) for e in range(2)]
    first_mine = send_all([out[0] for out in first], ring, -1)
    first_other = send_all([out[1] for out in first], ring, 1)
    cross = [run(e, [cross_mine[e], cross_other[e]]) for e in range(2)]
    pass_mine = send_all([out[0] for out in cross], ring, 1)
    pass_other = send_all([out[1] for out in cross], ring, -1)
    late = [run(e, [ahead_other[e], behind_mine[e]], jnp.float32) for e in range(2)]

    def add(*pieces):
        total = pieces[0].astype(jnp.float32)
        for piece in pieces[1:]:
            total = total + piece.astype(jnp.float32)
        return total.astype(bf16)

    last_other = send_all([add(late[e][0], pass_other[e]) for e in range(2)], ring, -1)
    last_mine = send_all([add(late[e][1], pass_mine[e]) for e in range(2)], ring, 1)
    swapped = send_all(
        [add(own[e][1], first_other[e], last_other[e]) for e in range(2)], far, 2
    )
    position = lax.axis_index("ep")
    pieces = pl.pallas_call(
        settle_kernel,
        in_specs=[pl.BlockSpec(memory_space=pltpu.SMEM)] + on_chip(8),
        out_specs=tuple(on_chip(groups)),
        out_shape=tuple(
            jax.ShapeDtypeStruct((experts_local, capacity, model_width), bf16)
            for _ in range(groups)
        ),
        compiler_params=grant(12),
        name="settle",
    )(
        position.astype(jnp.int32).reshape(1),
        own[0][0],
        own[1][0],
        first_mine[0],
        last_mine[0],
        swapped[0],
        first_mine[1],
        last_mine[1],
        swapped[1],
    )

    def toggle(mask):
        def move(y, c, z, x):
            place = (2 * y + c) ^ mask
            return (place // 2, place % 2, z, x)

        return hop(sizes, move)

    back = list(pieces)
    for k in (4, 5, 2, 3, 6, 7, 1):
        back[k] = send(pieces[k], toggle(k))
    place = ((expert_ids // experts_local) ^ position) * experts_local
    place = (place + expert_ids % experts_local) * capacity + slot_index
    combined = pl.pallas_call(
        combine_kernel,
        out_shape=jax.ShapeDtypeStruct((tokens, model_width), bf16),
        in_specs=on_chip(3 + groups),
        compiler_params=grant(12),
        name="combine",
    )(hidden, jnp.where(slot_index >= 0, place, -1).reshape(tokens, 2), gates, *back)
    return combined.reshape(frames_local, sites_local, model_width)


def solution(mesh):
    return jax.shard_map(
        block,
        mesh=mesh,
        in_specs=(
            P("ep", "tp", None, None),
            P("ep", "tp", None),
            P(),
            P("ep", "tp", None),
            P("ep", "tp", None),
            P("ep", "tp", None),
            P("ep", None, "tp"),
            P("ep", None, "tp"),
            P("ep", "tp", None),
        ),
        out_specs=P("ep", "tp", None),
        check_vma=False,
    )
```

```python
import math

import jax
import jax.numpy as jnp
from jax import lax
from jax.experimental import pallas as pl
from jax.experimental.pallas import tpu as pltpu
from jax.sharding import PartitionSpec as P


HD = 64
SITE_GROUP = 8
LANES = 2 * HD
SIDE = 4


def nt_dot(left, right):
    return lax.dot_general(
        left, right, (((1,), (1,)), ((), ())), preferred_element_type=jnp.float32
    )


def attend_kernel(qkv_ref, out_ref):
    sources, _, frames, sites, width = qkv_ref.shape
    rows = sources * frames * sites
    row_site = lax.broadcasted_iota(jnp.int32, (2 * rows, rows), 0) % sites
    col_site = lax.broadcasted_iota(jnp.int32, (2 * rows, rows), 1) % sites
    same_site = row_site == col_site
    low_head = lax.broadcasted_iota(jnp.int32, (rows, LANES), 1) < HD
    for pair in range(width // LANES):
        cols = pl.ds(pair * LANES, LANES)
        query = qkv_ref[:, 0, :, :, cols].reshape(rows, LANES)
        key = qkv_ref[:, 1, :, :, cols].reshape(rows, LANES)
        value = qkv_ref[:, 2, :, :, cols].reshape(rows, LANES)
        zero = jnp.zeros_like(query)
        both = jnp.concatenate(
            [jnp.where(low_head, query, zero), jnp.where(low_head, zero, query)], axis=0
        )
        scores = nt_dot(both, key) * (1.0 / math.sqrt(HD))
        scores = jnp.where(same_site, scores, -jnp.inf)
        expo = jnp.exp(scores - jnp.max(scores, axis=-1, keepdims=True))
        probs = (expo / jnp.sum(expo, axis=-1, keepdims=True)).astype(jnp.bfloat16)
        mixed = jnp.dot(probs, value, preferred_element_type=jnp.float32)
        mixed = jnp.where(low_head, mixed[:rows], mixed[rows:])
        out_ref[:, :, :, cols] = mixed.astype(out_ref.dtype).reshape(
            sources, frames, sites, LANES
        )


def route_kernel(att_ref, res_ref, gain_ref, target_ref, hidden_ref, rows_ref):
    _, frames, sites, half = att_ref.shape
    groups = att_ref.shape[0] // 2
    tokens = frames * groups * sites
    attended = jnp.concatenate(
        [
            jnp.concatenate(
                [
                    att_ref[2 * group + side, frame].astype(jnp.float32)
                    for frame in range(frames)
                    for group in range(groups)
                ],
                axis=0,
            )
            for side in range(2)
        ],
        axis=1,
    )
    hidden = res_ref[...].reshape(tokens, 2 * half).astype(jnp.float32) + attended
    hidden_ref[...] = hidden
    scale = lax.rsqrt(jnp.mean(hidden * hidden, axis=-1, keepdims=True) + 1e-06)
    normed = (hidden * scale * gain_ref[...]).astype(jnp.bfloat16)
    row = lax.broadcasted_iota(jnp.int32, (rows_ref.shape[0], tokens), 0)
    hit = (row == target_ref[0:1, :]) | (row == target_ref[1:2, :])
    picker = jnp.where(hit, 1.0, 0.0).astype(jnp.bfloat16)
    rows_ref[...] = jnp.dot(picker, normed, preferred_element_type=jnp.float32).astype(
        jnp.bfloat16
    )


def settle_kernel(position, *refs):
    own, moved, outs = refs[:2], refs[2:8], refs[8:]
    count = outs[0].shape[2]
    for k in range(2 * outs[0].shape[0]):
        start = pl.multiple_of((position[0] ^ k) * count, count)
        cut = pl.ds(start, count)
        for e in range(2):
            total = own[e][cut].astype(jnp.float32)
            for part in moved[3 * e : 3 * e + 3]:
                total = total + part[cut].astype(jnp.float32)
            outs[k % 2][k // 2, e] = total.astype(outs[0].dtype)


def join_kernel(left, right, *outs):
    for j, out in enumerate(outs):
        out[0] = left[j + 1]
        out[1] = right[j + 1]


def combine_kernel(hidden_ref, target_ref, gate_ref, *refs):
    left, right, *rest, out_ref = refs
    tokens, width = hidden_ref.shape
    blocks = [left[0], right[0]]
    for ref in rest:
        blocks += [ref[0], ref[1]]
    returned = jnp.concatenate([block[e] for block in blocks for e in range(2)], axis=0)
    col = lax.broadcasted_iota(jnp.int32, (tokens, returned.shape[0]), 1)
    moved = jnp.zeros((tokens, width), jnp.float32)
    for choice in range(2):
        target = target_ref[:, choice : choice + 1]
        picker = jnp.where(col == target, 1.0, 0.0).astype(jnp.bfloat16)
        weight = jnp.where(target >= 0, gate_ref[:, choice : choice + 1], 0.0)
        moved = moved + weight * jnp.dot(picker, returned, preferred_element_type=jnp.float32)
    out_ref[...] = (hidden_ref[...] + moved).astype(out_ref.dtype)


def mlp_kernel(pieces, *refs):
    weights = refs[pieces]
    outs = refs[pieces + 1 : -1]
    total = refs[-1]
    rows = jnp.concatenate([ref[...] for ref in refs[:pieces]], axis=0)
    total[...] = jnp.zeros(total.shape, total.dtype)

    @pl.loop(0, weights.shape[0])
    def _(i):
        gate_val = nt_dot(rows, weights[i, 0])
        up_val = nt_dot(rows, weights[i, 1])
        active = (gate_val / (1.0 + jnp.exp(-gate_val)) * up_val).astype(jnp.bfloat16)
        total[...] += jnp.dot(active, weights[i, 2], preferred_element_type=jnp.float32)

    count = total.shape[0] // pieces
    for i, out in enumerate(outs):
        out[...] = total[i * count : (i + 1) * count].astype(out.dtype)


def on_chip(count):
    return [pl.BlockSpec(memory_space=pltpu.VMEM)] * count


def grant(mebibytes):
    return pltpu.CompilerParams(vmem_limit_bytes=mebibytes << 20)


def mlp(pieces, dtype, weights):
    rows = sum(piece.shape[0] for piece in pieces)
    return pl.pallas_call(
        lambda *refs: mlp_kernel(len(pieces), *refs),
        in_specs=on_chip(len(pieces) + 1),
        out_specs=tuple(on_chip(len(pieces))),
        out_shape=tuple(jax.ShapeDtypeStruct(piece.shape, dtype) for piece in pieces),
        scratch_shapes=[pltpu.VMEM((rows, pieces[0].shape[1]), jnp.float32)],
        compiler_params=grant(18),
        name="mlp",
    )(*pieces, weights)


def pack_kernel(*refs):
    for i, source in enumerate(refs[:-1]):
        refs[-1][i] = source[...]


def pack(index, *sources):
    _, rows, width = sources[0].shape
    count = len(sources)
    steps = 2 * count
    return pl.pallas_call(
        pack_kernel,
        grid=(steps,),
        in_specs=[pl.BlockSpec((None, rows // steps, width), lambda i: (index, i, 0))] * count,
        out_specs=pl.BlockSpec((count, rows // steps, width), lambda i: (0, i, 0)),
        out_shape=jax.ShapeDtypeStruct((count, rows, width), sources[0].dtype),
        compiler_params=grant(58),
        name="pack",
    )(*sources)


def land_kernel(index, gate, up, down, near_gate, near_rest, out_ref, sem):
    sources = (
        (gate.at[index], up.at[index], down.at[index]),
        (near_gate.at[0], near_rest.at[0], near_rest.at[1]),
    )
    copies = [
        pltpu.make_async_copy(source, out_ref.at[i, j], sem.at[i, j])
        for i, group in enumerate(sources)
        for j, source in enumerate(group)
    ]
    for copy in copies:
        copy.start()
    for copy in copies:
        copy.wait()


def land(index, *sources):
    held = [pltpu.with_memory_space_constraint(source, pltpu.HBM) for source in sources]
    _, rows, width = sources[0].shape
    return pl.pallas_call(
        lambda *refs: land_kernel(index, *refs),
        in_specs=[pl.BlockSpec(memory_space=pltpu.HBM)] * len(held),
        out_specs=on_chip(1)[0],
        out_shape=pltpu.VMEM((2, 3, rows, width), sources[0].dtype),
        scratch_shapes=[pltpu.SemaphoreType.DMA((2, 3))],
        compiler_params=grant(11),
        name="land",
    )(*held)


def hop(sizes, move):
    count_y, count_z, count_x = sizes

    def index(y, c, z, x):
        return (
            ((y % count_y) * 2 + c) * (count_z * count_x)
            + (z % count_z) * count_x
            + x % count_x
        )

    return [
        (index(y, c, z, x), index(*move(y, c, z, x)))
        for y in range(count_y)
        for c in range(2)
        for z in range(count_z)
        for x in range(count_x)
    ]


def block(
    query_key_value, residual, norm_gain, expert_ids, route_gates, slot_index, w_gate, w_up, w_down
):
    frames_local, sites_local, model_width = residual.shape
    groups = lax.axis_size("ep")
    halves = 2
    site_groups = sites_local // SITE_GROUP
    assert site_groups * halves == groups
    half = model_width // halves
    tokens = frames_local * sites_local
    experts_local = w_gate.shape[0]
    experts_all = experts_local * groups
    capacity = 2 * tokens // experts_all
    bf16 = jnp.bfloat16

    spread = query_key_value.reshape(
        frames_local, site_groups, SITE_GROUP, 3, halves, half
    ).transpose(1, 4, 3, 0, 2, 5)
    spread = spread.reshape(groups, 3, frames_local, SITE_GROUP, half)
    gate = w_gate.transpose(0, 2, 1)
    up = w_up.transpose(0, 2, 1)
    together = lax.all_to_all(spread, "ep", split_axis=0, concat_axis=0, tiled=True)
    mixed = pl.pallas_call(
        attend_kernel,
        out_shape=jax.ShapeDtypeStruct((groups, frames_local, SITE_GROUP, half), bf16),
        in_specs=on_chip(1),
        compiler_params=grant(16),
        name="attend",
    )(together)
    attended = lax.all_to_all(mixed, "ep", split_axis=0, concat_axis=0, tiled=True)

    sizes = (groups // 2, SIDE, lax.axis_size("tp") // SIDE)

    def along_x(steps):
        return hop(sizes, lambda y, c, z, x: (y, c, z, x + steps))

    def along_z(steps):
        return hop(sizes, lambda y, c, z, x: (y, c, z + steps, x))

    def send(value, pairs):
        return lax.ppermute(value, ("ep", "tp"), pairs)

    beside = (
        hop(sizes, lambda y, c, z, x: (y, c, z, x - 1 + 2 * c)),
        hop(sizes, lambda y, c, z, x: (y, c, z - 1 + 2 * c, x)),
    )
    near = [[], []]
    for sources in ((gate,), (up, w_down)):
        for e in range(2):
            packed = pack(e, *sources)
            near[e].append(send(packed, beside[e]))
    weights = []
    for e in range(2):
        weights.append(land(e, gate, up, w_down, *near[e]))

    target = jnp.where(slot_index >= 0, expert_ids * capacity + slot_index, -1)
    target = target.reshape(tokens, 2)
    gates = route_gates.reshape(tokens, 2)
    slots = experts_all * capacity
    hidden, rows = pl.pallas_call(
        route_kernel,
        out_shape=(
            jax.ShapeDtypeStruct((tokens, model_width), jnp.float32),
            jax.ShapeDtypeStruct((slots, model_width), bf16),
        ),
        in_specs=on_chip(1) + [pl.BlockSpec()] + on_chip(2),
        out_specs=(pl.BlockSpec(), on_chip(1)[0]),
        compiler_params=grant(12),
        name="route",
    )(attended, residual, norm_gain.reshape(1, model_width), target.T)
    arrived = lax.all_to_all(
        rows.reshape(groups, experts_local, capacity, model_width),
        "ep",
        split_axis=0,
        concat_axis=0,
        tiled=True,
    )
    part_rows = groups * capacity
    mine = [arrived[:, e].reshape(part_rows, model_width) for e in range(2)]
    far = (along_x, along_z)
    ring = (along_z, along_x)

    def send_all(values, moves, steps):
        out = []
        for e in range(2):
            out.append(send(values[e], moves[e](steps)))
        return out

    done = ()

    def run(e, pieces, dtype=bf16):
        nonlocal done
        pieces, _ = lax.optimization_barrier((pieces, done))
        done = mlp(pieces, dtype, weights[e])
        return done

    other = send_all(mine, far, 2)
    ahead_mine = send_all(mine, ring, 1)
    behind_mine = send_all(mine, ring, -1)
    ahead_other = send_all(other, ring, 1)
    behind_other = send_all(other, ring, -1)
    cross_mine = send_all(ahead_mine, ring, 1)
    cross_other = send_all(behind_other, ring, -1)
    own = [run(e, [mine[e], other[e]]) for e in range(2)]
    first = [run(e, [ahead_mine[e], behind_other[e]]) for e in range(2)]
    first_mine = send_all([out[0] for out in first], ring, -1)
    first_other = send_all([out[1] for out in first], ring, 1)
    cross = [run(e, [cross_mine[e], cross_other[e]]) for e in range(2)]
    pass_mine = send_all([out[0] for out in cross], ring, 1)
    pass_other = send_all([out[1] for out in cross], ring, -1)
    late = [run(e, [ahead_other[e], behind_mine[e]], jnp.float32) for e in range(2)]

    def add(*pieces):
        total = pieces[0].astype(jnp.float32)
        for piece in pieces[1:]:
            total = total + piece.astype(jnp.float32)
        return total.astype(bf16)

    last_other = send_all([add(late[e][0], pass_other[e]) for e in range(2)], ring, -1
    )
    last_mine = send_all([add(late[e][1], pass_mine[e]) for e in range(2)], ring, 1
    )
    swapped = send_all([add(own[e][1], first_other[e], last_other[e]) for e in range(2)], far, 2
    )
    position = lax.axis_index("ep")
    pairs = groups // 2
    half_pieces = jax.ShapeDtypeStruct((pairs, experts_local, capacity, model_width), bf16)
    both_pieces = jax.ShapeDtypeStruct((2, experts_local, capacity, model_width), bf16)
    left, right = pl.pallas_call(
        settle_kernel,
        in_specs=[pl.BlockSpec(memory_space=pltpu.SMEM)] + on_chip(8),
        out_specs=tuple(on_chip(2)),
        out_shape=(half_pieces, half_pieces),
        compiler_params=grant(12),
        name="settle",
    )(
        position.astype(jnp.int32).reshape(1),
        own[0][0],
        own[1][0],
        first_mine[0],
        last_mine[0],
        swapped[0],
        first_mine[1],
        last_mine[1],
        swapped[1],
    )

    def toggle(mask):
        def move(y, c, z, x):
            place = (2 * y + c) ^ mask
            return (place // 2, place % 2, z, x)

        return hop(sizes, move)

    right = send(right, toggle(1))
    joined = pl.pallas_call(
        join_kernel,
        in_specs=on_chip(2),
        out_specs=tuple(on_chip(pairs - 1)),
        out_shape=(both_pieces,) * (pairs - 1),
        compiler_params=grant(6),
        name="join",
    )(left, right)
    back = []
    for j, value in enumerate(joined):
        back.append(send(value, toggle(2 * j + 2)))
    place = ((expert_ids // experts_local) ^ position) * experts_local
    place = (place + expert_ids % experts_local) * capacity + slot_index
    combined = pl.pallas_call(
        combine_kernel,
        out_shape=jax.ShapeDtypeStruct((tokens, model_width), bf16),
        in_specs=on_chip(5 + len(back)),
        compiler_params=grant(12),
        name="combine",
    )(hidden, jnp.where(slot_index >= 0, place, -1).reshape(tokens, 2), gates, left, right, *back)
    return combined.reshape(frames_local, sites_local, model_width)


def solution(mesh):
    return jax.shard_map(
        block,
        mesh=mesh,
        in_specs=(
            P("ep", "tp", None, None),
            P("ep", "tp", None),
            P(),
            P("ep", "tp", None),
            P("ep", "tp", None),
            P("ep", "tp", None),
            P("ep", None, "tp"),
            P("ep", None, "tp"),
            P("ep", "tp", None),
        ),
        out_specs=P("ep", "tp", None),
        check_vma=False,
    )
```
